256 devices in a mesh: dp: 32 (over x, y, core), mp: 8 (over z).
Axes of the slice: x: 4, y: 4, z: 8, core: 2. Of those that a mesh axis runs over, the one named last changes fastest.
Arguments:
- hidden: bfloat16 [49152, 5120], P('dp', 'mp'), may hold values from -6 to 6
- key_grads: bfloat16 [49152, 1024], P('dp', 'mp'), may hold values from -480 to 480
- token_ids: int32 [32, 1536], P('dp'), may hold values from 0 to 151643, as said below
- flags: int32 [32], P('dp'), may hold values from 0 to 2, as said below
- momentum: float32 [32, 5120, 1024], P('dp', 'mp'), may hold values from -8 to 8
- center: float32 [8, 640, 1024], P('mp', 'dp'), may hold values from -1.9 to 1.9
- weight: float32 [5120, 1024], P('mp'), may hold values from -0.078125 to 0.078125
Outputs:
- aggregate: float32 [8, 640, 1024], P('mp', 'dp')
- new_weight: float32 [5120, 1024], P('mp')
The draws below stay inside these ranges and needn't reach their ends.
Inputs may be any that keep to these rules, and one draw needn't show every extreme that they name: `token_ids`: each worker's batch holds 4 sequences of 384 positions; each sequence begins with at least 96 ids below 151643 and is filled up with 151643. `flags`: exactly 8 workers have a nonzero flag.
All inputs are finite; a program needn't handle non-finite values.
Results may differ from the reference program's by a relative error of at most 0.0003.
Values may be sent and summed in bfloat16 or wider, within the bound.
A program may use at most 64 MiB of HBM per device.

```python
import math
import jax
import jax.numpy as jnp
from jax import lax

D = 5120
KV = 1024
TOK_DEV = 1536
SEQ_LEN = 384
ITERS = 3
WORKERS = 32
BYZANTINE = 8
TOKENS = 49152
N_MP = 8


def draw_token_ids(key, part):
    base_key = jax.random.fold_in(key, 11)
    length_key, words_key = jax.random.split(base_key)
    sequences = TOK_DEV // SEQ_LEN
    lengths = jax.random.randint(length_key, (WORKERS, sequences, 1), SEQ_LEN // 4, SEQ_LEN + 1)
    position = jnp.arange(SEQ_LEN)[None, None, :]
    drawn_words = jax.random.randint(words_key, (WORKERS, sequences, SEQ_LEN), 0, 151643)
    filled = jnp.where(position < lengths, drawn_words, 151643)
    return filled.reshape(WORKERS, TOK_DEV).astype(jnp.int32)


def flag_values(key):
    base_key = jax.random.fold_in(key, 23)
    shuffle_key, kind_key = jax.random.split(base_key)
    shuffled = jax.random.permutation(shuffle_key, WORKERS)
    attack_kinds = jax.random.randint(kind_key, (WORKERS,), 1, 3)
    return jnp.where(shuffled < BYZANTINE, attack_kinds, 0).astype(jnp.int32)


def momentum_values(key):
    base_key = jax.random.fold_in(key, 37)
    worker_key, row_key, entry_key, shared_key = jax.random.split(base_key, 4)
    worker_scale = jnp.exp(jax.random.uniform(worker_key, (WORKERS, 1, 1), jnp.float32, math.log(0.1), math.log(0.6)))
    row_scale = jnp.exp(jax.random.uniform(row_key, (1, D, 1), jnp.float32, math.log(0.3), math.log(3.0)))
    noise = jnp.clip(jax.random.normal(entry_key, (WORKERS, D, KV), jnp.float32), -3.5, 3.5)
    shared = 0.25 * jnp.clip(jax.random.normal(shared_key, (1, D, KV), jnp.float32), -2.0, 2.0)
    return ((noise * worker_scale + shared) * row_scale).astype(jnp.float32)


def draw_flags(key, part):
    return flag_values(key)


def draw_momentum(key, part):
    return momentum_values(key)


def draw_center(key, part):
    values = momentum_values(key)
    honest = (flag_values(key) == 0).astype(jnp.float32)
    honest_mean = jnp.tensordot(honest / jnp.sum(honest), values, axes=1)
    noise_key = jax.random.fold_in(key, 53)
    noise = 0.03 * jnp.clip(jax.random.normal(noise_key, (D, KV), jnp.float32), -3.0, 3.0)
    drawn = jnp.clip(0.9 * honest_mean, -1.8, 1.8) + noise
    return drawn.reshape(N_MP, D // N_MP, KV).astype(jnp.float32)


def levels(own_key, extent, cuts, least, top_value):
    gain = 1.0
    for axis_at, blocks in cuts:
        steps = jax.random.uniform(jax.random.fold_in(jax.random.fold_in(own_key, 6), axis_at), (blocks,), jnp.float32, least / len(cuts), top_value / len(cuts))
        gain = gain * jnp.repeat(jnp.exp(steps), extent[axis_at] // blocks).reshape((-1,) + (1,) * (len(extent) - 1 - axis_at))
    return gain


def normal_values(stream_key, shape, scale, most, cuts=(), kind=jnp.bfloat16):
    array = scale * jax.random.normal(stream_key, shape, jnp.float32)
    if cuts:
        array = array * levels(stream_key, shape, cuts, -0.22, 0.18)
    return jnp.clip(array, -most, most).astype(kind)


def setup_inputs(seed: int = 0) -> dict:
    seeds = jax.random.split(jax.random.key(seed), 8)
    return {
        "hidden": normal_values(seeds[0], (TOKENS, D), 1.0, 6.0, ((0, 32), (1, 8))),
        "key_grads": normal_values(seeds[1], (TOKENS, KV), 80.0, 480.0, ((0, 32), (1, 8))),
        "token_ids": draw_token_ids(jax.random.fold_in(seeds[7], 71), 0),
        "flags": draw_flags(jax.random.fold_in(seeds[7], 71), 0),
        "momentum": draw_momentum(jax.random.fold_in(seeds[7], 71), 0),
        "center": draw_center(jax.random.fold_in(seeds[7], 71), 0),
        "weight": normal_values(seeds[6], (D, KV), D ** -0.5, 0.078125, ((0, 8),), jnp.float32),
    }


pad_token = 151643
momentum_beta = 0.9
attack_gain = 8.0
clip_ratio = 0.5
learning_rate = 0.05

def reference(hidden, key_grads, token_ids, flags, momentum, center, weight):

    def worker_momentum(index):
        rows = lax.dynamic_slice_in_dim(hidden, index * TOK_DEV, TOK_DEV, 0)
        grads = lax.dynamic_slice_in_dim(key_grads, index * TOK_DEV, TOK_DEV, 0)
        live = token_ids[index] != pad_token
        count = jnp.sum(live.astype(jnp.float32))
        masked = jnp.where(live[:, None], grads, jnp.zeros_like(grads))
        gradient = lax.dot_general(rows, masked, (((0,), (0,)), ((), ())), preferred_element_type=jnp.float32) / count
        blended = momentum_beta * momentum[index] + (1.0 - momentum_beta) * gradient
        factor = jnp.where(flags[index] == 1, attack_gain, jnp.where(flags[index] == 2, -1.0, 1.0))
        return blended * factor
    sent = lax.map(worker_momentum, jnp.arange(WORKERS, dtype=jnp.int32))
    current = center.reshape(D, KV)
    radius = clip_ratio * math.sqrt(D * KV)
    for iteration in range(ITERS):
        offsets = sent - current[None]
        distance = jnp.sqrt(lax.optimization_barrier(jnp.sum(offsets * offsets, axis=(1, 2))))
        weights_now = radius / jnp.maximum(distance, radius)
        current = current + lax.optimization_barrier(jnp.mean(weights_now[:, None, None] * offsets, axis=0))
    return (current.reshape(N_MP, D // N_MP, KV), weight - learning_rate * current)
```

```python
import math

import jax
import jax.numpy as jnp
from jax import lax
from jax.experimental import pallas as pl
from jax.experimental.pallas import tpu as pltpu
from jax.sharding import Mesh
from jax.sharding import PartitionSpec as P

D = 5120
KV = 1024
ITERS = 3
NX, NY, NC, NZ = 4, 4, 2, 8
DP = NX * NY * NC
ROWS = D // NZ
COLS = KV // NZ
GROUPS = 8
GR = ROWS // GROUPS
OWNED = ROWS // DP
TOK = 1536
NK = 4
TK = TOK // NK

pad_token = 151643
momentum_beta = 0.9
attack_gain = 8.0
clip_ratio = 0.5
learning_rate = 0.05
radius = clip_ratio * math.sqrt(D * KV)

MESH = pl.DeviceIdType.MESH
f32 = jnp.float32
bf16 = jnp.bfloat16
HIGHEST = lax.Precision.HIGHEST


def near_first():
    def far(i):
        return min(i, NX - i)

    pairs = [(i, j) for i in range(NX) for j in range(NY) if (i, j) != (0, 0)]
    return sorted(pairs, key=lambda p: far(p[0]) + far(p[1]))


def owner_of(group, b):
    x = group >> 1
    return x, 2 * (group & 1) + ((b + x) & 1)


def kernel(
    hid, kg, tok, flag, mom, cen, wgt,
    agg, nw,
    hid_v, ht, own_k, kbuf, mom_v, acc, out_v, recv, cen_r, cen_w, wgt_v, nw_v, vs, gz, gp, gam,
    load_sem, k_recv, k_send, a_recv, a_send, c_recv, c_send, gz_recv, gz_send, gp_recv, gp_send,
    v_recv, v_send, f_recv, f_send, nw_sem,
):
    x, y, c, z = (lax.axis_index(a) for a in ("x", "y", "c", "z"))
    chip = x * NY + y
    me = chip * NC + c
    up, down = (z + 1) & 7, (z + 7) & 7

    hid_load = pltpu.make_async_copy(hid, hid_v, load_sem.at[0])
    k_load = pltpu.make_async_copy(kg, own_k, load_sem.at[1])
    mom_load = pltpu.make_async_copy(mom.at[0], mom_v, load_sem.at[2])
    wgt_load = pltpu.make_async_copy(wgt, wgt_v, load_sem.at[3])
    hid_load.start()
    k_load.start()
    mom_load.start()

    barrier = pltpu.get_barrier_semaphore()

    def plane_id(i):
        return (i >> 3, (i >> 1) & 3, i & 1, z)

    @pl.loop(0, DP)
    def _(i):
        @pl.when(i != me)
        def _():
            pl.semaphore_signal(barrier, inc=1, device_id=plane_id(i), device_id_type=MESH)

    @pl.loop(0, NZ)
    def _(i):
        @pl.when(i != z)
        def _():
            pl.semaphore_signal(barrier, inc=1, device_id=(x, y, c, i), device_id_type=MESH)

    pl.semaphore_wait(barrier, DP - 1 + NZ - 1)

    def chunk_copy(src, j, k, way, dist, target):
        return pltpu.make_async_remote_copy(
            src_ref=src,
            dst_ref=kbuf.at[j * NK + k],
            send_sem=k_send.at[way],
            recv_sem=k_recv.at[way, dist, k],
            device_id=(x, y, c, target),
            device_id_type=MESH,
        )

    def kslice(j, k):
        return kbuf.at[j * NK + k]

    for k in range(NK):
        own = kg.at[pl.ds(k * TK, TK)]
        chunk_copy(own, z, k, 0, 0, up).start()
        chunk_copy(own, z, k, 1, 0, down).start()

    c_group = x * 2 + (y >> 1)
    quarter = (y & 1) * 2 + c
    for j in range(NZ):
        b, cc, slot = (j >> 1) & 1, j >> 2, j & 1
        tx, ty = owner_of(c_group, b)
        mine = (ty == y) & (c == cc)
        src = cen.at[0, :, pl.ds(j * COLS, COLS)]

        @pl.when(mine)
        def _():
            pltpu.make_async_copy(src, cen_r.at[slot, quarter], c_recv.at[slot, quarter]).start()

        @pl.when(jnp.logical_not(mine))
        def _():
            pltpu.make_async_remote_copy(
                src_ref=src,
                dst_ref=cen_r.at[slot, quarter],
                send_sem=c_send.at[j],
                recv_sem=c_recv.at[slot, quarter],
                device_id=(tx, ty, cc, z),
                device_id_type=MESH,
            ).start()

    wgt_load.start()

    live = (tok[...] != pad_token).astype(f32)
    count = jnp.sum(live)
    kind = flag[0]
    factor = jnp.where(kind == 1, attack_gain, jnp.where(kind == 2, -1.0, 1.0)).astype(f32)
    mom_scale = factor * momentum_beta
    grad_scale = factor * (1.0 - momentum_beta) / count
    mask = live.astype(bf16)

    hid_load.wait()
    for k in range(NK):
        part = jnp.transpose(hid_v[pl.ds(k * TK, TK), :])
        ht[k] = part * mask[:, k * TK:(k + 1) * TK]

    def finish(j, value):
        columns = pl.ds(pl.multiple_of(j * COLS, COLS), COLS)
        sent = mom_scale * mom_v[:, columns] + grad_scale * value
        out_v[pl.ds(j * GROUPS, GROUPS)] = sent.reshape(GROUPS, GR, COLS)
        b, cc, slot = (j >> 1) & 1, j >> 2, j & 1

        @pl.loop(0, GROUPS)
        def _(group):
            tx, ty = owner_of(group, b)
            mine = (tx == x) & (ty == y) & (cc == c)

            @pl.when(mine)
            def _():
                pltpu.make_async_copy(
                    out_v.at[j * GROUPS + group], recv.at[slot, me], a_recv.at[slot]
                ).start()

            @pl.when(jnp.logical_not(mine))
            def _():
                pltpu.make_async_remote_copy(
                    src_ref=out_v.at[j * GROUPS + group],
                    dst_ref=recv.at[slot, me],
                    send_sem=a_send,
                    recv_sem=a_recv.at[slot],
                    device_id=(tx, ty, cc, z),
                    device_id_type=MESH,
                ).start()

    k_load.wait()
    mom_load.wait()
    acc[:, :COLS] = jnp.dot(ht[0], own_k[:TK], preferred_element_type=f32)
    for k in range(1, NK):
        acc[:, :COLS] += jnp.dot(ht[k], own_k[k * TK:(k + 1) * TK], preferred_element_type=f32)
    finish(z, acc[:, :COLS])

    @pl.loop(0, 3 * NK)
    def _(t):
        dist, k = 1 + (t >> 2), t & 3
        j_up, j_down = (z - dist + 8) & 7, (z + dist) & 7
        arrived = chunk_copy(kslice(j_up, k), j_up, k, 0, dist - 1, up)
        arrived.wait_recv()

        @pl.when((dist < 3) | (k < 2))
        def _():
            chunk_copy(kslice(j_up, k), j_up, k, 0, dist, up).start()

        arrived = chunk_copy(kslice(j_down, k), j_down, k, 1, dist - 1, down)
        arrived.wait_recv()

        @pl.when((dist < 3) | (k >= 2))
        def _():
            chunk_copy(kslice(j_down, k), j_down, k, 1, dist, down).start()

        both = jnp.concatenate([kbuf[j_up * NK + k], kbuf[j_down * NK + k]], axis=1)
        product = jnp.dot(ht[k], both, preferred_element_type=f32)

        @pl.when(k == 0)
        def _():
            acc[...] = product

        @pl.when(k > 0)
        def _():
            acc[...] += product

        @pl.when(k == NK - 1)
        def _():
            finish(j_up, acc[:, :COLS])
            finish(j_down, acc[:, COLS:])

    far = (z + 4) & 7
    for k in range(2):
        chunk_copy(kslice(far, k), far, k, 0, 3, up).wait_recv()
        chunk_copy(kslice(far, k + 2), far, k + 2, 1, 3, down).wait_recv()
        part = jnp.dot(ht[k], kbuf[far * NK + k], preferred_element_type=f32)
        part += jnp.dot(ht[k + 2], kbuf[far * NK + k + 2], preferred_element_type=f32)
        if k == 0:
            acc[:, :COLS] = part
        else:
            acc[:, :COLS] += part
    finish(far, acc[:, :COLS])

    for slot in range(2):
        for q in range(4):
            pltpu.make_async_copy(cen_r.at[slot, q], cen_r.at[slot, q], c_recv.at[slot, q]).wait()
            cen_w[slot, q * OWNED:(q + 1) * OWNED, :] = cen_r[slot, q]

    first = (z + 1) & 1
    gram = None
    for turn in range(2):
        slot = (first + turn) & 1
        pltpu.make_async_copy(recv.at[slot], recv.at[slot], a_recv.at[slot]).wait()

        def body(i, total):
            halves = []
            for h in range(2):
                r = pl.ds(pl.multiple_of(i * 16 + h * 8, 8), 8)
                offset = recv[slot, :, r, :] - cen_w[slot, r, :][None]
                halves.append(offset.reshape(DP * 8, COLS))
            both = jnp.concatenate(halves, axis=1)
            hi = both.astype(bf16)
            lo = (both - hi.astype(f32)).astype(bf16)
            nt = (((1,), (1,)), ((), ()))
            total = total + lax.dot_general(hi, hi, nt, preferred_element_type=f32)
            total = total + lax.dot_general(hi, lo, nt, preferred_element_type=f32)
            total = total + lax.dot_general(lo, hi, nt, preferred_element_type=f32)
            return total

        start = jnp.zeros((DP * 8, DP * 8), f32) if gram is None else gram
        gram = lax.fori_loop(0, GR // 16, body, start)

    ii = lax.broadcasted_iota(jnp.int32, (DP * 8, DP * 8), 0)
    jj = lax.broadcasted_iota(jnp.int32, (DP * 8, DP * 8), 1)
    gram = jnp.where((ii & 7) == (jj & 7), gram, 0.0)
    gram = jnp.sum(gram.reshape(DP, 8, DP * 8), axis=1)
    fold = (
        (lax.broadcasted_iota(jnp.int32, (DP * 8, COLS), 0) >> 3)
        == lax.broadcasted_iota(jnp.int32, (DP * 8, COLS), 1)
    ).astype(f32)
    gram = jnp.dot(gram, fold, precision=HIGHEST, preferred_element_type=f32)
    packed = gram[0:8]
    for q in range(1, 4):
        packed = packed + pltpu.roll(gram[q * 8:(q + 1) * 8], q * DP, 1)

    gz[z] = packed

    @pl.loop(1, NZ)
    def _(i):
        pltpu.make_async_remote_copy(
            src_ref=gz.at[z],
            dst_ref=gz.at[z],
            send_sem=gz_send,
            recv_sem=gz_recv,
            device_id=(x, y, c, (z + i) & 7),
            device_id_type=MESH,
        ).start()

    pltpu.make_async_copy(gz.at[pl.ds(0, NZ - 1)], gz.at[pl.ds(0, NZ - 1)], gz_recv).wait()
    gp[me] = jnp.sum(gz[...], axis=0)

    @pl.loop(1, DP)
    def _(i):
        pltpu.make_async_remote_copy(
            src_ref=gp.at[me],
            dst_ref=gp.at[me],
            send_sem=gp_send,
            recv_sem=gp_recv,
            device_id=plane_id((me + i) & (DP - 1)),
            device_id_type=MESH,
        ).start()

    pltpu.make_async_copy(gp.at[pl.ds(0, DP - 1)], gp.at[pl.ds(0, DP - 1)], gp_recv).wait()
    packed = jnp.sum(gp[...], axis=0)
    lane8 = lax.broadcasted_iota(jnp.int32, (8, COLS), 1)
    pieces = []
    for q in range(4):
        piece = packed if q == 0 else pltpu.roll(packed, COLS - q * DP, 1)
        pieces.append(jnp.where(lane8 < DP, piece, 0.0))
    gram = jnp.concatenate(pieces, axis=0)

    row = lax.broadcasted_iota(jnp.int32, (DP, COLS), 0)
    lane = lax.broadcasted_iota(jnp.int32, (DP, COLS), 1)
    diag = jnp.where(row == lane, gram, 0.0)
    diag_col = jnp.sum(diag, axis=1, keepdims=True)
    diag_row = jnp.sum(diag, axis=0, keepdims=True)
    in_row = lane[:1] < DP
    w_col = jnp.zeros((DP, 1), f32)
    w_row = jnp.zeros((1, COLS), f32)
    for iteration in range(ITERS):
        if iteration == 0:
            sq_col, sq_row = diag_col, diag_row
        else:
            g_col = jnp.sum(gram * w_row, axis=1, keepdims=True)
            g_row = jnp.sum(gram * w_col, axis=0, keepdims=True)
            quad = jnp.sum(g_row * w_row, axis=1, keepdims=True)
            sq_col = diag_col - 2.0 * g_col + quad
            sq_row = diag_row - 2.0 * g_row + quad
        coef_col = radius / jnp.maximum(jnp.sqrt(jnp.maximum(sq_col, 0.0)), radius)
        coef_row = radius / jnp.maximum(jnp.sqrt(jnp.maximum(sq_row, 0.0)), radius)
        coef_row = jnp.where(in_row, coef_row, 0.0)
        mean = jnp.sum(coef_row, axis=1, keepdims=True) * (1.0 / DP)
        w_col = (1.0 - mean) * w_col + coef_col * (1.0 / DP)
        w_row = (1.0 - mean) * w_row + coef_row * (1.0 / DP)
    gam[...] = jnp.broadcast_to(w_col, (DP, COLS))
    keep = 1.0 - jnp.sum(w_row, axis=1, keepdims=True)

    for slot in range(2):
        total = keep * cen_w[slot]
        for w in range(DP):
            total = total + gam[w:w + 1, :] * recv[slot, w]
        vs[c, chip, slot] = total

    order = near_first()
    for dx, dy in order:
        pltpu.make_async_remote_copy(
            src_ref=vs.at[c, chip],
            dst_ref=vs.at[c, chip],
            send_sem=v_send,
            recv_sem=v_recv.at[chip],
            device_id=((x + dx) & 3, (y + dy) & 3, c, z),
            device_id_type=MESH,
        ).start()

    wgt_load.wait()

    def forward(p):
        return pltpu.make_async_remote_copy(
            src_ref=vs.at[c, p],
            dst_ref=vs.at[c, p],
            send_sem=f_send,
            recv_sem=f_recv.at[p],
            device_id=(x, y, 1 - c, z),
            device_id_type=MESH,
        )

    def place(core, p):
        px, py = p >> 2, p & 3
        rows = pl.ds(pl.multiple_of((px * 2 + (py >> 1)) * GR, GR), GR)
        half = 2 * core + ((px + py) & 1)
        for slot in range(2):
            columns = pl.ds(pl.multiple_of(half * 2 * COLS + slot * COLS, COLS), COLS)
            nw_v[rows, columns] = wgt_v[rows, columns] - learning_rate * vs[core, p, slot]
        both = pl.ds(pl.multiple_of(half * 2 * COLS, 2 * COLS), 2 * COLS)
        pltpu.make_async_copy(nw_v.at[rows, both], nw.at[rows, both], nw_sem).start()

    forward(chip).start()
    place(c, chip)
    for dx, dy in order:
        p = ((x - dx) & 3) * NY + ((y - dy) & 3)
        pltpu.make_async_copy(vs.at[c, p], vs.at[c, p], v_recv.at[p]).wait()
        forward(p).start()
        place(c, p)
    for dx, dy in [(0, 0)] + order:
        p = ((x - dx) & 3) * NY + ((y - dy) & 3)
        pltpu.make_async_copy(vs.at[1 - c, p], vs.at[1 - c, p], f_recv.at[p]).wait()
        place(1 - c, p)

    for cc in range(NC):
        for b in range(2):
            px, py = owner_of(c_group, b)
            for slot in range(2):
                j = cc * 4 + b * 2 + slot
                for q in range(4):
                    @pl.when(quarter == q)
                    def _():
                        agg[0, :, j * COLS:(j + 1) * COLS] = vs[
                            cc, px * NY + py, slot, q * OWNED:(q + 1) * OWNED, :
                        ]

    pltpu.make_async_copy(nw_v, nw, nw_sem).wait()
    for way in range(2):
        part = kbuf.at[pl.ds(0, 14)]
        pltpu.make_async_copy(part, part, k_send.at[way]).wait()
    sent = out_v.at[pl.ds(0, NZ * GROUPS - 2)]
    pltpu.make_async_copy(sent, sent, a_send).wait()
    for j in range(NZ):
        tx, ty = owner_of(c_group, (j >> 1) & 1)

        @pl.when(jnp.logical_not((ty == y) & (c == (j >> 2))))
        def _():
            pltpu.make_async_copy(cen_r.at[0, 0], cen_r.at[0, 0], c_send.at[j]).wait()
    pltpu.make_async_copy(gz.at[pl.ds(0, NZ - 1)], gz.at[pl.ds(0, NZ - 1)], gz_send).wait()
    pltpu.make_async_copy(gp.at[pl.ds(0, DP - 1)], gp.at[pl.ds(0, DP - 1)], gp_send).wait()
    pltpu.make_async_copy(vs.at[0, pl.ds(0, 15)], vs.at[0, pl.ds(0, 15)], v_send).wait()
    pltpu.make_async_copy(vs.at[0], vs.at[0], f_send).wait()


def per_device(hidden, key_grads, token_ids, flags, momentum, center, weight):
    hbm = pl.BlockSpec(memory_space=pl.ANY)
    vmem = pl.BlockSpec(memory_space=pltpu.VMEM)
    dma = pltpu.SemaphoreType.DMA
    return pl.pallas_call(
        kernel,
        out_shape=(
            jax.ShapeDtypeStruct((1, OWNED, KV), f32),
            jax.ShapeDtypeStruct((ROWS, KV), f32),
        ),
        in_specs=[hbm, hbm, vmem, pl.BlockSpec(memory_space=pltpu.SMEM), hbm, hbm, hbm],
        out_specs=(vmem, hbm),
        scratch_shapes=[
            pltpu.VMEM((TOK, ROWS), bf16),
            pltpu.VMEM((NK, ROWS, TK), bf16),
            pltpu.VMEM((TOK, COLS), bf16),
            pltpu.VMEM((NZ * NK, TK, COLS), bf16),
            pltpu.VMEM((ROWS, KV), f32),
            pltpu.VMEM((ROWS, 2 * COLS), f32),
            pltpu.VMEM((NZ * GROUPS, GR, COLS), f32),
            pltpu.VMEM((2, DP, GR, COLS), f32),
            pltpu.VMEM((2, 4, OWNED, COLS), f32),
            pltpu.VMEM((2, GR, COLS), f32),
            pltpu.VMEM((ROWS, KV), f32),
            pltpu.VMEM((ROWS, KV), f32),
            pltpu.VMEM((NC, NX * NY, 2, GR, COLS), f32),
            pltpu.VMEM((NZ, 8, COLS), f32),
            pltpu.VMEM((DP, 8, COLS), f32),
            pltpu.VMEM((DP, COLS), f32),
            dma((4,)),
            dma((2, 4, NK)),
            dma((2,)),
            dma((2,)),
            dma,
            dma((2, 4)),
            dma((NZ,)),
            dma,
            dma,
            dma,
            dma,
            dma((NX * NY,)),
            dma,
            dma((NX * NY,)),
            dma,
            dma,
        ],
        compiler_params=pltpu.CompilerParams(collective_id=0, has_side_effects=True),
        name="clip",
    )(hidden, key_grads, token_ids, flags, momentum, center, weight)


def solution(mesh):
    torus = Mesh(mesh.devices.reshape(NX, NY, NC, NZ), ("x", "y", "c", "z"))
    dp = ("x", "y", "c")
    return jax.shard_map(
        per_device,
        mesh=torus,
        in_specs=(
            P(dp, "z"),
            P(dp, "z"),
            P(dp, None),
            P(dp),
            P(dp, "z", None),
            P("z", dp, None),
            P("z", None),
        ),
        out_specs=(P("z", dp, None), P("z", None)),
        check_vma=False,
    )
```

```python
import math

import jax
import jax.numpy as jnp
from jax import lax
from jax.experimental import pallas as pl
from jax.experimental.pallas import tpu as pltpu
from jax.sharding import Mesh
from jax.sharding import PartitionSpec as P

D = 5120
KV = 1024
ITERS = 3
NX, NY, NC, NZ = 4, 4, 2, 8
DP = NX * NY * NC
ROWS = D // NZ
COLS = KV // NZ
GROUPS = 8
GR = ROWS // GROUPS
OWNED = ROWS // DP
TOK = 1536
NK = 4
TK = TOK // NK

pad_token = 151643
momentum_beta = 0.9
attack_gain = 8.0
clip_ratio = 0.5
learning_rate = 0.05
radius = clip_ratio * math.sqrt(D * KV)

MESH = pl.DeviceIdType.MESH
f32 = jnp.float32
bf16 = jnp.bfloat16
i16 = jnp.int16
MR = GR + 8
HIGHEST = lax.Precision.HIGHEST


def near_first():
    def far(i):
        return min(i, NX - i)

    pairs = [(i, j) for i in range(NX) for j in range(NY) if (i, j) != (0, 0)]
    return sorted(pairs, key=lambda p: far(p[0]) + far(p[1]))


def encode(values):
    top = jnp.max(jnp.abs(values), axis=1, keepdims=True)
    code = jnp.ceil(256.0 * jnp.log2(jnp.maximum(top, 2.0 ** -100)) + 0.0625)
    steps = jnp.round(values * (32767.0 / jnp.exp2(code * (1.0 / 256.0))))
    code = jnp.broadcast_to(code, (values.shape[0], 8, COLS))
    return steps.astype(jnp.int32).astype(i16), code.astype(jnp.int32).astype(i16)


def step_of(code):
    return jnp.exp2(code.astype(jnp.int32).astype(f32) * (1.0 / 256.0)) * (1.0 / 32767.0)


def owner_of(group, b):
    x = group >> 1
    return x, 2 * (group & 1) + ((b + x) & 1)


def kernel(
    hid, kg, tok, flag, mom, cen, wgt,
    agg, nw,
hid_v, ht, own_k, cen_v, cen_j, kbuf, mom_v, acc, out_v, recv, scl, cen_r, cen_w, wgt_v, nw_v, vs, gz, gp, gam,
    load_sem, k_recv, k_send, a_recv, a_send, c_recv, c_send, gz_recv, gz_send, gp_recv, gp_send,
    v_recv, v_send, f_recv, f_send, nw_sem,
):
    x, y, c, z = (lax.axis_index(a) for a in ("x", "y", "c", "z"))
    chip = x * NY + y
    me = chip * NC + c
    up, down = (z + 1) & 7, (z + 7) & 7

    hid_load = pltpu.make_async_copy(hid, hid_v, load_sem.at[0])
    k_load = pltpu.make_async_copy(kg, own_k, load_sem.at[1])
    mom_load = pltpu.make_async_copy(mom.at[0], mom_v, load_sem.at[2])
    cen_load = pltpu.make_async_copy(cen, cen_v, load_sem.at[4])
    wgt_load = pltpu.make_async_copy(wgt, wgt_v, load_sem.at[3])
    cen_load.start()
    hid_load.start()
    k_load.start()
    mom_load.start()

    barrier = pltpu.get_barrier_semaphore()

    def plane_id(i):
        return (i >> 3, (i >> 1) & 3, i & 1, z)

    @pl.loop(0, DP)
    def _(i):
        @pl.when(i != me)
        def _():
            pl.semaphore_signal(barrier, inc=1, device_id=plane_id(i), device_id_type=MESH)

    @pl.loop(0, NZ)
    def _(i):
        @pl.when(i != z)
        def _():
            pl.semaphore_signal(barrier, inc=1, device_id=(x, y, c, i), device_id_type=MESH)

    pl.semaphore_wait(barrier, DP - 1 + NZ - 1)

    def chunk_copy(src, j, k, way, dist, target):
        return pltpu.make_async_remote_copy(
            src_ref=src,
            dst_ref=kbuf.at[j * NK + k],
            send_sem=k_send.at[way],
            recv_sem=k_recv.at[way, dist, k],
            device_id=(x, y, c, target),
            device_id_type=MESH,
        )

    def kslice(j, k):
        return kbuf.at[j * NK + k]

    for k in range(NK):
        own = kg.at[pl.ds(k * TK, TK)]
        chunk_copy(own, z, k, 0, 0, up).start()
        chunk_copy(own, z, k, 1, 0, down).start()

    c_group = x * 2 + (y >> 1)
    quarter = (y & 1) * 2 + c
    cen_load.wait()
    for j in range(NZ):
        cen_j[j] = cen_v[:, j, :]
    for j in range(NZ):
        b, cc, slot = (j >> 1) & 1, j >> 2, j & 1
        tx, ty = owner_of(c_group, b)
        mine = (ty == y) & (c == cc)
        src = cen_j.at[j]

        @pl.when(mine)
        def _():
            pltpu.make_async_copy(src, cen_r.at[slot, quarter], c_recv.at[slot, quarter]).start()

        @pl.when(jnp.logical_not(mine))
        def _():
            pltpu.make_async_remote_copy(
                src_ref=src,
                dst_ref=cen_r.at[slot, quarter],
                send_sem=c_send.at[j],
                recv_sem=c_recv.at[slot, quarter],
                device_id=(tx, ty, cc, z),
                device_id_type=MESH,
            ).start()

    wgt_load.start()

    live = (tok[...] != pad_token).astype(f32)
    count = jnp.sum(live)
    kind = flag[0]
    factor = jnp.where(kind == 1, attack_gain, jnp.where(kind == 2, -1.0, 1.0)).astype(f32)
    mom_scale = factor * momentum_beta
    grad_scale = factor * (1.0 - momentum_beta) / count
    mask = live.astype(bf16)

    hid_load.wait()
    for k in range(NK):
        part = jnp.transpose(hid_v[pl.ds(k * TK, TK), :])
        ht[k] = part * mask[:, k * TK:(k + 1) * TK]

    def finish(j, value):
        columns = pl.ds(pl.multiple_of(j * COLS, COLS), COLS)
        sent = mom_scale * mom_v[:, columns] + grad_scale * value
        steps, code = encode(sent.reshape(GROUPS, GR, COLS))
        out_v[pl.ds(j * GROUPS, GROUPS), :GR] = steps
        out_v[pl.ds(j * GROUPS, GROUPS), GR:] = code
        b, cc, slot = (j >> 1) & 1, j >> 2, j & 1

        @pl.loop(0, GROUPS)
        def _(group):
            tx, ty = owner_of(group, b)
            mine = (tx == x) & (ty == y) & (cc == c)

            @pl.when(mine)
            def _():
                pltpu.make_async_copy(
                    out_v.at[j * GROUPS + group], recv.at[slot, me], a_recv.at[slot]
                ).start()

            @pl.when(jnp.logical_not(mine))
            def _():
                pltpu.make_async_remote_copy(
                    src_ref=out_v.at[j * GROUPS + group],
                    dst_ref=recv.at[slot, me],
                    send_sem=a_send,
                    recv_sem=a_recv.at[slot],
                    device_id=(tx, ty, cc, z),
                    device_id_type=MESH,
                ).start()

    k_load.wait()
    mom_load.wait()
    acc[:, :COLS] = jnp.dot(ht[0], own_k[:TK], preferred_element_type=f32)
    for k in range(1, NK):
        acc[:, :COLS] += jnp.dot(ht[k], own_k[k * TK:(k + 1) * TK], preferred_element_type=f32)
    finish(z, acc[:, :COLS])

    @pl.loop(0, 3 * NK)
    def _(t):
        dist, k = 1 + (t >> 2), t & 3
        j_up, j_down = (z - dist + 8) & 7, (z + dist) & 7
        arrived = chunk_copy(kslice(j_up, k), j_up, k, 0, dist - 1, up)
        arrived.wait_recv()

        @pl.when((dist < 3) | (k < 2))
        def _():
            chunk_copy(kslice(j_up, k), j_up, k, 0, dist, up).start()

        arrived = chunk_copy(kslice(j_down, k), j_down, k, 1, dist - 1, down)
        arrived.wait_recv()

        @pl.when((dist < 3) | (k >= 2))
        def _():
            chunk_copy(kslice(j_down, k), j_down, k, 1, dist, down).start()

        both = jnp.concatenate([kbuf[j_up * NK + k], kbuf[j_down * NK + k]], axis=1)
        product = jnp.dot(ht[k], both, preferred_element_type=f32)

        @pl.when(k == 0)
        def _():
            acc[...] = product

        @pl.when(k > 0)
        def _():
            acc[...] += product

        @pl.when(k == NK - 1)
        def _():
            finish(j_up, acc[:, :COLS])
            finish(j_down, acc[:, COLS:])

    far = (z + 4) & 7
    for k in range(2):
        chunk_copy(kslice(far, k), far, k, 0, 3, up).wait_recv()
        chunk_copy(kslice(far, k + 2), far, k + 2, 1, 3, down).wait_recv()
        part = jnp.dot(ht[k], kbuf[far * NK + k], preferred_element_type=f32)
        part += jnp.dot(ht[k + 2], kbuf[far * NK + k + 2], preferred_element_type=f32)
        if k == 0:
            acc[:, :COLS] = part
        else:
            acc[:, :COLS] += part
    finish(far, acc[:, :COLS])

    for slot in range(2):
        for q in range(4):
            pltpu.make_async_copy(cen_r.at[slot, q], cen_r.at[slot, q], c_recv.at[slot, q]).wait()
            cen_w[slot, q * OWNED:(q + 1) * OWNED, :] = cen_r[slot, q]

    first = (z + 1) & 1
    gram = None
    for turn in range(2):
        slot = (first + turn) & 1
        pltpu.make_async_copy(recv.at[slot], recv.at[slot], a_recv.at[slot]).wait()

        scl[slot] = step_of(recv[slot, :, GR:, :])

        def body(i, total):
            halves = []
            for h in range(2):
                r = pl.ds(pl.multiple_of(i * 16 + h * 8, 8), 8)
                steps = recv[slot, :, r, :].astype(jnp.int32).astype(f32)
                offset = steps * scl[slot] - cen_w[slot, r, :][None]
                halves.append(offset.reshape(DP * 8, COLS))
            both = jnp.concatenate(halves, axis=1)
            hi = both.astype(bf16)
            lo = (both - hi.astype(f32)).astype(bf16)
            nt = (((1,), (1,)), ((), ()))
            total = total + lax.dot_general(hi, hi, nt, preferred_element_type=f32)
            total = total + lax.dot_general(hi, lo, nt, preferred_element_type=f32)
            total = total + lax.dot_general(lo, hi, nt, preferred_element_type=f32)
            return total

        start = jnp.zeros((DP * 8, DP * 8), f32) if gram is None else gram
        gram = lax.fori_loop(0, GR // 16, body, start)

    ii = lax.broadcasted_iota(jnp.int32, (DP * 8, DP * 8), 0)
    jj = lax.broadcasted_iota(jnp.int32, (DP * 8, DP * 8), 1)
    gram = jnp.where((ii & 7) == (jj & 7), gram, 0.0)
    gram = jnp.sum(gram.reshape(DP, 8, DP * 8), axis=1)
    fold = (
        (lax.broadcasted_iota(jnp.int32, (DP * 8, COLS), 0) >> 3)
        == lax.broadcasted_iota(jnp.int32, (DP * 8, COLS), 1)
    ).astype(f32)
    gram = jnp.dot(gram, fold, precision=HIGHEST, preferred_element_type=f32)
    packed = gram[0:8]
    for q in range(1, 4):
        packed = packed + pltpu.roll(gram[q * 8:(q + 1) * 8], q * DP, 1)

    gz[z] = packed

    @pl.loop(1, NZ)
    def _(i):
        pltpu.make_async_remote_copy(
            src_ref=gz.at[z],
            dst_ref=gz.at[z],
            send_sem=gz_send,
            recv_sem=gz_recv,
            device_id=(x, y, c, (z + i) & 7),
            device_id_type=MESH,
        ).start()

    pltpu.make_async_copy(gz.at[pl.ds(0, NZ - 1)], gz.at[pl.ds(0, NZ - 1)], gz_recv).wait()
    gp[me] = jnp.sum(gz[...], axis=0)

    @pl.loop(1, DP)
    def _(i):
        pltpu.make_async_remote_copy(
            src_ref=gp.at[me],
            dst_ref=gp.at[me],
            send_sem=gp_send,
            recv_sem=gp_recv,
            device_id=plane_id((me + i) & (DP - 1)),
            device_id_type=MESH,
        ).start()

    pltpu.make_async_copy(gp.at[pl.ds(0, DP - 1)], gp.at[pl.ds(0, DP - 1)], gp_recv).wait()
    packed = jnp.sum(gp[...], axis=0)
    lane8 = lax.broadcasted_iota(jnp.int32, (8, COLS), 1)
    pieces = []
    for q in range(4):
        piece = packed if q == 0 else pltpu.roll(packed, COLS - q * DP, 1)
        pieces.append(jnp.where(lane8 < DP, piece, 0.0))
    gram = jnp.concatenate(pieces, axis=0)

    row = lax.broadcasted_iota(jnp.int32, (DP, COLS), 0)
    lane = lax.broadcasted_iota(jnp.int32, (DP, COLS), 1)
    diag = jnp.where(row == lane, gram, 0.0)
    diag_col = jnp.sum(diag, axis=1, keepdims=True)
    diag_row = jnp.sum(diag, axis=0, keepdims=True)
    in_row = lane[:1] < DP
    w_col = jnp.zeros((DP, 1), f32)
    w_row = jnp.zeros((1, COLS), f32)
    for iteration in range(ITERS):
        if iteration == 0:
            sq_col, sq_row = diag_col, diag_row
        else:
            g_col = jnp.sum(gram * w_row, axis=1, keepdims=True)
            g_row = jnp.sum(gram * w_col, axis=0, keepdims=True)
            quad = jnp.sum(g_row * w_row, axis=1, keepdims=True)
            sq_col = diag_col - 2.0 * g_col + quad
            sq_row = diag_row - 2.0 * g_row + quad
        coef_col = radius / jnp.maximum(jnp.sqrt(jnp.maximum(sq_col, 0.0)), radius)
        coef_row = radius / jnp.maximum(jnp.sqrt(jnp.maximum(sq_row, 0.0)), radius)
        coef_row = jnp.where(in_row, coef_row, 0.0)
        mean = jnp.sum(coef_row, axis=1, keepdims=True) * (1.0 / DP)
        w_col = (1.0 - mean) * w_col + coef_col * (1.0 / DP)
        w_row = (1.0 - mean) * w_row + coef_row * (1.0 / DP)
    gam[...] = jnp.broadcast_to(w_col, (DP, COLS))
    keep = 1.0 - jnp.sum(w_row, axis=1, keepdims=True)

    for slot in range(2):
        total = (keep * cen_w[slot]).reshape(GR // 8, 8, COLS)
        for w in range(DP):
            steps = recv[slot, w, :GR].astype(jnp.int32).astype(f32).reshape(GR // 8, 8, COLS)
            total = total + (gam[w:w + 1, :] * scl[slot, w])[None] * steps
        steps, code = encode(total.reshape(1, GR, COLS))
        vs[c, chip, slot, :GR] = steps[0]
        vs[c, chip, slot, GR:] = code[0]

    order = near_first()
    for dx, dy in order:
        pltpu.make_async_remote_copy(
            src_ref=vs.at[c, chip],
            dst_ref=vs.at[c, chip],
            send_sem=v_send,
            recv_sem=v_recv.at[chip],
            device_id=((x + dx) & 3, (y + dy) & 3, c, z),
            device_id_type=MESH,
        ).start()

    wgt_load.wait()

    def forward(p):
        return pltpu.make_async_remote_copy(
            src_ref=vs.at[c, p],
            dst_ref=vs.at[c, p],
            send_sem=f_send,
            recv_sem=f_recv.at[p],
            device_id=(x, y, 1 - c, z),
            device_id_type=MESH,
        )

    def decode(core, p, slot):
        steps = vs[core, p, slot, :GR].astype(jnp.int32).astype(f32).reshape(GR // 8, 8, COLS)
        return (steps * step_of(vs[core, p, slot, GR:])[None]).reshape(GR, COLS)

    def place(core, p):
        px, py = p >> 2, p & 3
        rows = pl.ds(pl.multiple_of((px * 2 + (py >> 1)) * GR, GR), GR)
        half = 2 * core + ((px + py) & 1)
        for slot in range(2):
            columns = pl.ds(pl.multiple_of(half * 2 * COLS + slot * COLS, COLS), COLS)
            nw_v[rows, columns] = wgt_v[rows, columns] - learning_rate * decode(core, p, slot)
        both = pl.ds(pl.multiple_of(half * 2 * COLS, 2 * COLS), 2 * COLS)
        pltpu.make_async_copy(nw_v.at[rows, both], nw.at[rows, both], nw_sem).start()

    forward(chip).start()
    place(c, chip)
    for dx, dy in order:
        p = ((x - dx) & 3) * NY + ((y - dy) & 3)
        pltpu.make_async_copy(vs.at[c, p], vs.at[c, p], v_recv.at[p]).wait()
        forward(p).start()
        place(c, p)
    for dx, dy in [(0, 0)] + order:
        p = ((x - dx) & 3) * NY + ((y - dy) & 3)
        pltpu.make_async_copy(vs.at[1 - c, p], vs.at[1 - c, p], f_recv.at[p]).wait()
        place(1 - c, p)

    for cc in range(NC):
        for b in range(2):
            px, py = owner_of(c_group, b)
            for slot in range(2):
                j = cc * 4 + b * 2 + slot
                rows = decode(cc, px * NY + py, slot)
                for q in range(4):
                    @pl.when(quarter == q)
                    def _():
                        agg[:, j, :] = rows[q * OWNED:(q + 1) * OWNED]

    pltpu.make_async_copy(nw_v, nw, nw_sem).wait()
    for way in range(2):
        part = kbuf.at[pl.ds(0, 14)]
        pltpu.make_async_copy(part, part, k_send.at[way]).wait()
    sent = out_v.at[pl.ds(0, NZ * GROUPS - 2)]
    pltpu.make_async_copy(sent, sent, a_send).wait()
    for j in range(NZ):
        tx, ty = owner_of(c_group, (j >> 1) & 1)

        @pl.when(jnp.logical_not((ty == y) & (c == (j >> 2))))
        def _():
            pltpu.make_async_copy(cen_r.at[0, 0], cen_r.at[0, 0], c_send.at[j]).wait()
    pltpu.make_async_copy(gz.at[pl.ds(0, NZ - 1)], gz.at[pl.ds(0, NZ - 1)], gz_send).wait()
    pltpu.make_async_copy(gp.at[pl.ds(0, DP - 1)], gp.at[pl.ds(0, DP - 1)], gp_send).wait()
    pltpu.make_async_copy(vs.at[0, pl.ds(0, 15)], vs.at[0, pl.ds(0, 15)], v_send).wait()
    pltpu.make_async_copy(vs.at[0], vs.at[0], f_send).wait()


def per_device(hidden, key_grads, token_ids, flags, momentum, center, weight):
    hidden, key_grads, momentum, center, weight = (
        pltpu.with_memory_space_constraint(a, pltpu.HBM)
        for a in (hidden, key_grads, momentum, center.reshape(OWNED, NZ, COLS), weight)
    )
    hbm = pl.BlockSpec(memory_space=pltpu.HBM)
    anywhere = pl.BlockSpec(memory_space=pl.ANY)
    vmem = pl.BlockSpec(memory_space=pltpu.VMEM)
    dma = pltpu.SemaphoreType.DMA
    aggregate, new_weight = pl.pallas_call(
        kernel,
        out_shape=(
            jax.ShapeDtypeStruct((OWNED, NZ, COLS), f32),
            jax.ShapeDtypeStruct((ROWS, KV), f32),
        ),
        in_specs=[hbm, hbm, vmem, pl.BlockSpec(memory_space=pltpu.SMEM), hbm, hbm, hbm],
        out_specs=(vmem, anywhere),
        scratch_shapes=[
            pltpu.VMEM((TOK, ROWS), bf16),
            pltpu.VMEM((NK, ROWS, TK), bf16),
            pltpu.VMEM((TOK, COLS), bf16),
            pltpu.VMEM((OWNED, NZ, COLS), f32),
            pltpu.VMEM((NZ, OWNED, COLS), f32),
            pltpu.VMEM((NZ * NK, TK, COLS), bf16),
            pltpu.VMEM((ROWS, KV), f32),
            pltpu.VMEM((ROWS, 2 * COLS), f32),
            pltpu.VMEM((NZ * GROUPS, MR, COLS), i16),
            pltpu.VMEM((2, DP, MR, COLS), i16),
            pltpu.VMEM((2, DP, 8, COLS), f32),
            pltpu.VMEM((2, 4, OWNED, COLS), f32),
            pltpu.VMEM((2, GR, COLS), f32),
            pltpu.VMEM((ROWS, KV), f32),
            pltpu.VMEM((ROWS, KV), f32),
            pltpu.VMEM((NC, NX * NY, 2, MR, COLS), i16),
            pltpu.VMEM((NZ, 8, COLS), f32),
            pltpu.VMEM((DP, 8, COLS), f32),
            pltpu.VMEM((DP, COLS), f32),
            dma((5,)),
            dma((2, 4, NK)),
            dma((2,)),
            dma((2,)),
            dma,
            dma((2, 4)),
            dma((NZ,)),
            dma,
            dma,
            dma,
            dma,
            dma((NX * NY,)),
            dma,
            dma((NX * NY,)),
            dma,
            dma,
        ],
        compiler_params=pltpu.CompilerParams(collective_id=0, has_side_effects=True, vmem_limit_bytes=40 * 1024 * 1024),
        name="clip",
    )(hidden, key_grads, token_ids, flags, momentum, center, weight)
    return aggregate.reshape(1, OWNED, KV), new_weight


def solution(mesh):
    torus = Mesh(mesh.devices.reshape(NX, NY, NC, NZ), ("x", "y", "c", "z"))
    dp = ("x", "y", "c")
    return jax.shard_map(
        per_device,
        mesh=torus,
        in_specs=(
            P(dp, "z"),
            P(dp, "z"),
            P(dp, None),
            P(dp),
            P(dp, "z", None),
            P("z", dp, None),
            P("z", None),
        ),
        out_specs=(P("z", dp, None), P("z", None)),
        check_vma=False,
    )
```

```python
import math

import jax
import jax.numpy as jnp
from jax import lax
from jax.experimental import pallas as pl
from jax.experimental.pallas import tpu as pltpu
from jax.sharding import Mesh
from jax.sharding import PartitionSpec as P

D = 5120
KV = 1024
ITERS = 3
NX, NY, NC, NZ = 4, 4, 2, 8
DP = NX * NY * NC
ROWS = D // NZ
COLS = KV // NZ
GROUPS = 8
GR = ROWS // GROUPS
OWNED = ROWS // DP
TOK = 1536
NK = 4
TK = TOK // NK

pad_token = 151643
momentum_beta = 0.9
attack_gain = 8.0
clip_ratio = 0.5
learning_rate = 0.05
radius = clip_ratio * math.sqrt(D * KV)

MESH = pl.DeviceIdType.MESH
f32 = jnp.float32
bf16 = jnp.bfloat16
i16 = jnp.int16
MR = GR + 8
HIGHEST = lax.Precision.HIGHEST


def encode(values):
    top = jnp.max(jnp.abs(values), axis=1, keepdims=True)
    code = jnp.ceil(256.0 * jnp.log2(jnp.maximum(top, 2.0 ** -100)) + 0.0625)
    steps = jnp.round(values * (32767.0 / jnp.exp2(code * (1.0 / 256.0))))
    code = jnp.broadcast_to(code, (values.shape[0], 8, COLS))
    return steps.astype(jnp.int32).astype(i16), code.astype(jnp.int32).astype(i16)


def step_of(code):
    return jnp.exp2(code.astype(jnp.int32).astype(f32) * (1.0 / 256.0)) * (1.0 / 32767.0)


def owner_of(group, b):
    x = group >> 1
    return x, 2 * (group & 1) + ((b + x) & 1)


def kernel(
    hid, kg, tok, flag, mom, cen, wgt,
    agg, nw,
    tok_v, hid_v, ht, own_k, cen_v, cen_j, kbuf, mom_v, acc, out_v, recv, scl, cen_r, cen_w, wgt_v, nw_v, vs, gx, gy, gz, agg_v, gam,
    load_sem, k_recv, k_send, a_recv, a_send, c_recv, c_send, g_recv, g_send,
    v_recv, v_send, f_recv, f_send, nw_sem, here,
):
    x, y, c, z = (lax.axis_index(a) for a in ("x", "y", "c", "z"))
    chip = x * NY + y
    me = chip * NC + c
    up, down = (z + 1) & 7, (z + 7) & 7

    hid_load = pltpu.make_async_copy(hid, hid_v, load_sem.at[0])
    k_load = pltpu.make_async_copy(kg, own_k, load_sem.at[1])
    mom_load = pltpu.make_async_copy(mom.at[0], mom_v, load_sem.at[2])
    cen_load = pltpu.make_async_copy(cen, cen_v, load_sem.at[4])
    tok_load = pltpu.make_async_copy(tok, tok_v, load_sem.at[5])
    wgt_load = pltpu.make_async_copy(wgt, wgt_v, load_sem.at[3])
    cen_load.start()
    tok_load.start()
    hid_load.start()
    k_load.start()
    mom_load.start()

    barrier = pltpu.get_barrier_semaphore()

    beside_x = [((x + d) & 3, y, c, z) for d in (1, 3)]
    beside_y = [(x, (y + d) & 3, c, z) for d in (1, 3)]
    beside_z = [(x, y, c, up), (x, y, c, down)]
    partner = (x, y, 1 - c, z)
    for other in beside_z + beside_x + beside_y + [partner]:
        pl.semaphore_signal(barrier, inc=1, device_id=other, device_id_type=MESH)
    pl.semaphore_wait(barrier, 7)

    def tell(i, others):
        for other in others:
            pl.semaphore_signal(here.at[i], inc=1, device_id=other, device_id_type=MESH)

    def hear(i, others):
        pl.semaphore_wait(here.at[i], len(others))

    def chunk_copy(src, j, k, way, dist, target):
        return pltpu.make_async_remote_copy(
            src_ref=src,
            dst_ref=kbuf.at[j * NK + k],
            send_sem=k_send.at[way],
            recv_sem=k_recv.at[way, dist, k],
            device_id=(x, y, c, target),
            device_id_type=MESH,
        )

    def kslice(j, k):
        return kbuf.at[j * NK + k]

    for k in range(NK):
        own = kg.at[pl.ds(k * TK, TK)]
        chunk_copy(own, z, k, 0, 0, up).start()
        chunk_copy(own, z, k, 1, 0, down).start()

    tell(0, beside_x)

    c_group = x * 2 + (y >> 1)
    quarter = (y & 1) * 2 + c
    cen_load.wait()
    for j in range(NZ):
        cen_j[j] = cen_v[:, j, :]
    hear(0, beside_x)
    tell(1, beside_y)
    wgt_load.start()
    tok_load.wait()

    live = (tok_v[...] != pad_token).astype(f32)
    count = jnp.sum(live)
    kind = flag[0]
    factor = jnp.where(kind == 1, attack_gain, jnp.where(kind == 2, -1.0, 1.0)).astype(f32)
    mom_scale = factor * momentum_beta
    grad_scale = factor * (1.0 - momentum_beta) / count
    mask = live.astype(bf16)

    hid_load.wait()
    hear(1, beside_y)
    tell(2, beside_y)
    for k in range(NK):
        part = jnp.transpose(hid_v[pl.ds(k * TK, TK), :])
        ht[k] = part * mask[:, k * TK:(k + 1) * TK]

    hear(2, beside_y)
    tell(3, [partner])

    def finish(j, value):
        columns = pl.ds(pl.multiple_of(j * COLS, COLS), COLS)
        sent = mom_scale * mom_v[:, columns] + grad_scale * value
        steps, code = encode(sent.reshape(GROUPS, GR, COLS))
        out_v[pl.ds(j * GROUPS, GROUPS), :GR] = steps
        out_v[pl.ds(j * GROUPS, GROUPS), GR:] = code
        b, cc, slot = (j >> 1) & 1, j >> 2, j & 1

        @pl.loop(0, GROUPS)
        def _(group):
            tx, ty = owner_of(group, b)
            mine = (tx == x) & (ty == y) & (cc == c)

            @pl.when(mine)
            def _():
                pltpu.make_async_copy(
                    out_v.at[j * GROUPS + group], recv.at[slot, me], a_recv.at[slot]
                ).start()

            @pl.when(jnp.logical_not(mine))
            def _():
                pltpu.make_async_remote_copy(
                    src_ref=out_v.at[j * GROUPS + group],
                    dst_ref=recv.at[slot, me],
                    send_sem=a_send,
                    recv_sem=a_recv.at[slot],
                    device_id=(tx, ty, cc, z),
                    device_id_type=MESH,
                ).start()

    k_load.wait()
    mom_load.wait()
    acc[:, :COLS] = jnp.dot(ht[0], own_k[:TK], preferred_element_type=f32)
    for k in range(1, NK):
        acc[:, :COLS] += jnp.dot(ht[k], own_k[k * TK:(k + 1) * TK], preferred_element_type=f32)
    hear(3, [partner])

    for j in range(NZ):
        b, cc, slot = (j >> 1) & 1, j >> 2, j & 1
        tx, ty = owner_of(c_group, b)
        mine = (ty == y) & (c == cc)
        src = cen_j.at[j]

        @pl.when(mine)
        def _():
            pltpu.make_async_copy(src, cen_r.at[slot, quarter], c_recv.at[slot, quarter]).start()

        @pl.when(jnp.logical_not(mine))
        def _():
            pltpu.make_async_remote_copy(
                src_ref=src,
                dst_ref=cen_r.at[slot, quarter],
                send_sem=c_send.at[j],
                recv_sem=c_recv.at[slot, quarter],
                device_id=(tx, ty, cc, z),
                device_id_type=MESH,
            ).start()

    finish(z, acc[:, :COLS])

    @pl.loop(0, 3 * NK)
    def _(t):
        dist, k = 1 + (t >> 2), t & 3
        j_up, j_down = (z - dist + 8) & 7, (z + dist) & 7
        arrived = chunk_copy(kslice(j_up, k), j_up, k, 0, dist - 1, up)
        arrived.wait_recv()

        @pl.when((dist < 3) | (k < 2))
        def _():
            chunk_copy(kslice(j_up, k), j_up, k, 0, dist, up).start()

        arrived = chunk_copy(kslice(j_down, k), j_down, k, 1, dist - 1, down)
        arrived.wait_recv()

        @pl.when((dist < 3) | (k >= 2))
        def _():
            chunk_copy(kslice(j_down, k), j_down, k, 1, dist, down).start()

        both = jnp.concatenate([kbuf[j_up * NK + k], kbuf[j_down * NK + k]], axis=1)
        product = jnp.dot(ht[k], both, preferred_element_type=f32)

        @pl.when(k == 0)
        def _():
            acc[...] = product

        @pl.when(k > 0)
        def _():
            acc[...] += product

        @pl.when(k == NK - 1)
        def _():
            finish(j_up, acc[:, :COLS])
            finish(j_down, acc[:, COLS:])

    far = (z + 4) & 7
    for k in range(2):
        chunk_copy(kslice(far, k), far, k, 0, 3, up).wait_recv()
        chunk_copy(kslice(far, k + 2), far, k + 2, 1, 3, down).wait_recv()
        part = jnp.dot(ht[k], kbuf[far * NK + k], preferred_element_type=f32)
        part += jnp.dot(ht[k + 2], kbuf[far * NK + k + 2], preferred_element_type=f32)
        if k == 0:
            acc[:, :COLS] = part
        else:
            acc[:, :COLS] += part
    finish(far, acc[:, :COLS])

    for slot in range(2):
        for q in range(4):
            pltpu.make_async_copy(cen_r.at[slot, q], cen_r.at[slot, q], c_recv.at[slot, q]).wait()
            cen_w[slot, q * OWNED:(q + 1) * OWNED, :] = cen_r[slot, q]

    first = (z + 1) & 1
    gram = None
    for turn in range(2):
        slot = (first + turn) & 1
        pltpu.make_async_copy(recv.at[slot], recv.at[slot], a_recv.at[slot]).wait()

        scl[slot] = step_of(recv[slot, :, GR:, :])

        def body(i, total):
            halves = []
            for h in range(2):
                r = pl.ds(pl.multiple_of(i * 16 + h * 8, 8), 8)
                steps = recv[slot, :, r, :].astype(jnp.int32).astype(f32)
                offset = steps * scl[slot] - cen_w[slot, r, :][None]
                halves.append(offset.reshape(DP * 8, COLS))
            both = jnp.concatenate(halves, axis=1)
            hi = both.astype(bf16)
            lo = (both - hi.astype(f32)).astype(bf16)
            nt = (((1,), (1,)), ((), ()))
            total = total + lax.dot_general(hi, hi, nt, preferred_element_type=f32)
            total = total + lax.dot_general(hi, lo, nt, preferred_element_type=f32)
            total = total + lax.dot_general(lo, hi, nt, preferred_element_type=f32)
            return total

        start = jnp.zeros((DP * 8, DP * 8), f32) if gram is None else gram
        gram = lax.fori_loop(0, GR // 16, body, start)

    ii = lax.broadcasted_iota(jnp.int32, (DP * 8, DP * 8), 0)
    jj = lax.broadcasted_iota(jnp.int32, (DP * 8, DP * 8), 1)
    gram = jnp.where((ii & 7) == (jj & 7), gram, 0.0)
    gram = jnp.sum(gram.reshape(DP, 8, DP * 8), axis=1)
    fold = (
        (lax.broadcasted_iota(jnp.int32, (DP * 8, COLS), 0) >> 3)
        == lax.broadcasted_iota(jnp.int32, (DP * 8, COLS), 1)
    ).astype(f32)
    gram = jnp.dot(gram, fold, precision=HIGHEST, preferred_element_type=f32)
    packed = gram[0:8]
    for q in range(1, 4):
        packed = packed + pltpu.roll(gram[q * 8:(q + 1) * 8], q * DP, 1)

    def reduce(stage, buffer, own, count, place_of):
        buffer[own] = packed

        @pl.loop(1, count)
        def _(i):
            pltpu.make_async_remote_copy(
                src_ref=buffer.at[own],
                dst_ref=buffer.at[own],
                send_sem=g_send.at[stage],
                recv_sem=g_recv.at[stage],
                device_id=place_of((own + i) & (count - 1)),
                device_id_type=MESH,
            ).start()

        others = buffer.at[pl.ds(0, count - 1)]
        pltpu.make_async_copy(others, others, g_recv.at[stage]).wait()
        return jnp.sum(buffer[...], axis=0)

    packed = reduce(0, gx, x * 2 + c, NX * NC, lambda i: (i >> 1, y, i & 1, z))
    packed = reduce(1, gy, y, NY, lambda i: (x, i, c, z))
    packed = reduce(2, gz, z, NZ, lambda i: (x, y, c, i))
    lane8 = lax.broadcasted_iota(jnp.int32, (8, COLS), 1)
    pieces = []
    for q in range(4):
        piece = packed if q == 0 else pltpu.roll(packed, COLS - q * DP, 1)
        pieces.append(jnp.where(lane8 < DP, piece, 0.0))
    gram = jnp.concatenate(pieces, axis=0)

    row = lax.broadcasted_iota(jnp.int32, (DP, COLS), 0)
    lane = lax.broadcasted_iota(jnp.int32, (DP, COLS), 1)
    diag = jnp.where(row == lane, gram, 0.0)
    diag_col = jnp.sum(diag, axis=1, keepdims=True)
    diag_row = jnp.sum(diag, axis=0, keepdims=True)
    in_row = lane[:1] < DP
    w_col = jnp.zeros((DP, 1), f32)
    w_row = jnp.zeros((1, COLS), f32)
    for iteration in range(ITERS):
        if iteration == 0:
            sq_col, sq_row = diag_col, diag_row
        else:
            g_col = jnp.sum(gram * w_row, axis=1, keepdims=True)
            g_row = jnp.sum(gram * w_col, axis=0, keepdims=True)
            quad = jnp.sum(g_row * w_row, axis=1, keepdims=True)
            sq_col = diag_col - 2.0 * g_col + quad
            sq_row = diag_row - 2.0 * g_row + quad
        coef_col = radius / jnp.maximum(jnp.sqrt(jnp.maximum(sq_col, 0.0)), radius)
        coef_row = radius / jnp.maximum(jnp.sqrt(jnp.maximum(sq_row, 0.0)), radius)
        coef_row = jnp.where(in_row, coef_row, 0.0)
        mean = jnp.sum(coef_row, axis=1, keepdims=True) * (1.0 / DP)
        w_col = (1.0 - mean) * w_col + coef_col * (1.0 / DP)
        w_row = (1.0 - mean) * w_row + coef_row * (1.0 / DP)
    gam[...] = jnp.broadcast_to(w_col, (DP, COLS))
    keep = 1.0 - jnp.sum(w_row, axis=1, keepdims=True)

    for slot in range(2):
        total = (keep * cen_w[slot]).reshape(GR // 8, 8, COLS)
        for w in range(DP):
            steps = recv[slot, w, :GR].astype(jnp.int32).astype(f32).reshape(GR // 8, 8, COLS)
            total = total + (gam[w:w + 1, :] * scl[slot, w])[None] * steps
        steps, code = encode(total.reshape(1, GR, COLS))
        vs[c, chip, slot, :GR] = steps[0]
        vs[c, chip, slot, GR:] = code[0]

    ring = (1, 3, 2)

    def chip_at(first, second, sign):
        cx = (x + sign * (first * (1 - c) + second * c)) & 3
        cy = (y + sign * (first * c + second * (1 - c))) & 3
        return cx, cy

    def send(p, first, second):
        pltpu.make_async_remote_copy(
            src_ref=vs.at[c, p],
            dst_ref=vs.at[c, p],
            send_sem=v_send,
            recv_sem=v_recv.at[p],
            device_id=(*chip_at(first, second, 1), c, z),
            device_id_type=MESH,
        ).start()

    def source(first, second):
        px, py = chip_at(first, second, -1)
        return px * NY + py

    def arrive(p):
        pltpu.make_async_copy(vs.at[c, p], vs.at[c, p], v_recv.at[p]).wait()

    for s in ring:
        send(chip, s, 0)
    for s in ring:
        send(chip, 0, s)
    wgt_load.wait()

    def forward(p):
        return pltpu.make_async_remote_copy(
            src_ref=vs.at[c, p],
            dst_ref=vs.at[c, p],
            send_sem=f_send,
            recv_sem=f_recv.at[p],
            device_id=(x, y, 1 - c, z),
            device_id_type=MESH,
        )

    def decode(core, p, slot):
        steps = vs[core, p, slot, :GR].astype(jnp.int32).astype(f32).reshape(GR // 8, 8, COLS)
        return (steps * step_of(vs[core, p, slot, GR:])[None]).reshape(GR, COLS)

    def place(core, p):
        px, py = p >> 2, p & 3
        rows = pl.ds(pl.multiple_of((px * 2 + (py >> 1)) * GR, GR), GR)
        half = 2 * core + ((px + py) & 1)
        for slot in range(2):
            columns = pl.ds(pl.multiple_of(half * 2 * COLS + slot * COLS, COLS), COLS)
            nw_v[rows, columns] = wgt_v[rows, columns] - learning_rate * decode(core, p, slot)
        both = pl.ds(pl.multiple_of(half * 2 * COLS, 2 * COLS), 2 * COLS)
        pltpu.make_async_copy(nw_v.at[rows, both], nw.at[rows, both], nw_sem).start()

    forward(chip).start()
    for s in ring:
        p = source(s, 0)
        arrive(p)
        for t in ring:
            send(p, 0, t)
        forward(p).start()
    for s in (0,) + ring:
        place(c, source(s, 0))
    for s in (0,) + ring:
        for t in ring:
            p = source(s, t)
            arrive(p)
            forward(p).start()
            place(c, p)
    for s in (0,) + ring:
        for t in (0,) + ring:
            p = source(t, s)
            pltpu.make_async_copy(vs.at[1 - c, p], vs.at[1 - c, p], f_recv.at[p]).wait()
            place(1 - c, p)

    for cc in range(NC):
        for b in range(2):
            px, py = owner_of(c_group, b)
            for slot in range(2):
                j = cc * 4 + b * 2 + slot
                rows = decode(cc, px * NY + py, slot)
                for q in range(4):
                    @pl.when(quarter == q)
                    def _():
                        agg_v[:, j, :] = rows[q * OWNED:(q + 1) * OWNED]

    agg_out = pltpu.make_async_copy(agg_v, agg, load_sem.at[4])
    agg_out.start()

    agg_out.wait()
    pltpu.make_async_copy(nw_v, nw, nw_sem).wait()
    for way in range(2):
        part = kbuf.at[pl.ds(0, 14)]
        pltpu.make_async_copy(part, part, k_send.at[way]).wait()
    sent = out_v.at[pl.ds(0, NZ * GROUPS - 2)]
    pltpu.make_async_copy(sent, sent, a_send).wait()
    for j in range(NZ):
        tx, ty = owner_of(c_group, (j >> 1) & 1)

        @pl.when(jnp.logical_not((ty == y) & (c == (j >> 2))))
        def _():
            pltpu.make_async_copy(cen_r.at[0, 0], cen_r.at[0, 0], c_send.at[j]).wait()
    for stage, buffer, count in ((0, gx, NX * NC), (1, gy, NY), (2, gz, NZ)):
        others = buffer.at[pl.ds(0, count - 1)]
        pltpu.make_async_copy(others, others, g_send.at[stage]).wait()
    pltpu.make_async_copy(vs.at[c, pl.ds(0, 15)], vs.at[c, pl.ds(0, 15)], v_send).wait()
    pltpu.make_async_copy(vs.at[c], vs.at[c], f_send).wait()


def per_device(hidden, key_grads, token_ids, flags, momentum, center, weight):
    hidden, key_grads, token_ids, momentum, center, weight = (
        pltpu.with_memory_space_constraint(a, pltpu.HBM)
        for a in (hidden, key_grads, token_ids, momentum, center.reshape(OWNED, NZ, COLS), weight)
    )
    hbm = pl.BlockSpec(memory_space=pltpu.HBM)
    anywhere = pl.BlockSpec(memory_space=pl.ANY)
    dma = pltpu.SemaphoreType.DMA
    aggregate, new_weight = pl.pallas_call(
        kernel,
        out_shape=(
            jax.ShapeDtypeStruct((OWNED, NZ, COLS), f32),
            jax.ShapeDtypeStruct((ROWS, KV), f32),
        ),
        in_specs=[hbm, hbm, hbm, pl.BlockSpec(memory_space=pltpu.SMEM), hbm, hbm, hbm],
        out_specs=(anywhere, anywhere),
        scratch_shapes=[
            pltpu.VMEM((1, TOK), jnp.int32),
            pltpu.VMEM((TOK, ROWS), bf16),
            pltpu.VMEM((NK, ROWS, TK), bf16),
            pltpu.VMEM((TOK, COLS), bf16),
            pltpu.VMEM((OWNED, NZ, COLS), f32),
            pltpu.VMEM((NZ, OWNED, COLS), f32),
            pltpu.VMEM((NZ * NK, TK, COLS), bf16),
            pltpu.VMEM((ROWS, KV), f32),
            pltpu.VMEM((ROWS, 2 * COLS), f32),
            pltpu.VMEM((NZ * GROUPS, MR, COLS), i16),
            pltpu.VMEM((2, DP, MR, COLS), i16),
            pltpu.VMEM((2, DP, 8, COLS), f32),
            pltpu.VMEM((2, 4, OWNED, COLS), f32),
            pltpu.VMEM((2, GR, COLS), f32),
            pltpu.VMEM((ROWS, KV), f32),
            pltpu.VMEM((ROWS, KV), f32),
            pltpu.VMEM((NC, NX * NY, 2, MR, COLS), i16),
            pltpu.VMEM((NX * NC, 8, COLS), f32),
            pltpu.VMEM((NY, 8, COLS), f32),
            pltpu.VMEM((NZ, 8, COLS), f32),
            pltpu.VMEM((OWNED, NZ, COLS), f32),
            pltpu.VMEM((DP, COLS), f32),
            dma((6,)),
            dma((2, 4, NK)),
            dma((2,)),
            dma((2,)),
            dma,
            dma((2, 4)),
            dma((NZ,)),
            dma((3,)),
            dma((3,)),
            dma((NX * NY,)),
            dma,
            dma((NX * NY,)),
            dma,
            dma,
            pltpu.SemaphoreType.REGULAR((4,)),
        ],
        compiler_params=pltpu.CompilerParams(collective_id=0, has_side_effects=True, vmem_limit_bytes=40 * 1024 * 1024),
        name="clip",
    )(hidden, key_grads, token_ids, flags, momentum, center, weight)
    return aggregate.reshape(1, OWNED, KV), new_weight


def solution(mesh):
    torus = Mesh(mesh.devices.reshape(NX, NY, NC, NZ), ("x", "y", "c", "z"))
    dp = ("x", "y", "c")
    return jax.shard_map(
        per_device,
        mesh=torus,
        in_specs=(
            P(dp, "z"),
            P(dp, "z"),
            P(dp, None),
            P(dp),
            P(dp, "z", None),
            P("z", dp, None),
            P("z", None),
        ),
        out_specs=(P("z", dp, None), P("z", None)),
        check_vma=False,
    )
```

```python
import math

import jax
import jax.numpy as jnp
from jax import lax
from jax.experimental import pallas as pl
from jax.experimental.pallas import tpu as pltpu
from jax.sharding import Mesh
from jax.sharding import PartitionSpec as P

D = 5120
KV = 1024
ITERS = 3
NX, NY, NC, NZ = 4, 4, 2, 8
DP = NX * NY * NC
ROWS = D // NZ
COLS = KV // NZ
GROUPS = 8
GR = ROWS // GROUPS
OWNED = ROWS // DP
TOK = 1536
NK = 4
TK = TOK // NK

pad_token = 151643
momentum_beta = 0.9
attack_gain = 8.0
clip_ratio = 0.5
learning_rate = 0.05
radius = clip_ratio * math.sqrt(D * KV)

MESH = pl.DeviceIdType.MESH
f32 = jnp.float32
bf16 = jnp.bfloat16
i16 = jnp.int16
MR = GR + 8
HIGHEST = lax.Precision.HIGHEST


def encode(values):
    top = jnp.max(jnp.abs(values), axis=1, keepdims=True)
    code = jnp.ceil(256.0 * jnp.log2(jnp.maximum(top, 2.0 ** -100)) + 0.0625)
    steps = jnp.round(values * (32767.0 / jnp.exp2(code * (1.0 / 256.0))))
    code = jnp.broadcast_to(code, (values.shape[0], 8, COLS))
    return steps.astype(jnp.int32).astype(i16), code.astype(jnp.int32).astype(i16)


def step_of(code):
    return jnp.exp2(code.astype(jnp.int32).astype(f32) * (1.0 / 256.0)) * (1.0 / 32767.0)


def owner_of(group, b):
    x = group >> 1
    return x, 2 * (group & 1) + ((b + x) & 1)


def kernel(
    hid, kg, tok, flag, mom, cen, wgt,
    agg, nw,
    tok_v, hid_v, ht, own_k, cen_v, cen_j, kbuf, mom_v, acc, out_v, recv, scl, cen_r, cen_w, wgt_v, nw_v, vs, gx, gy, gz, agg_v, gam,
    load_sem, k_recv, k_send, a_recv, a_send, c_recv, c_send, g_recv, g_send,
    v_recv, v_send, f_recv, f_send, nw_sem, here,
):
    x, y, c, z = (lax.axis_index(a) for a in ("x", "y", "c", "z"))
    chip = x * NY + y
    me = chip * NC + c
    up, down = (z + 1) & 7, (z + 7) & 7

    hid_load = pltpu.make_async_copy(hid, hid_v, load_sem.at[0])
    k_load = pltpu.make_async_copy(kg, own_k, load_sem.at[1])
    mom_load = pltpu.make_async_copy(mom.at[0], mom_v, load_sem.at[2])
    cen_load = pltpu.make_async_copy(cen, cen_v, load_sem.at[4])
    tok_load = pltpu.make_async_copy(tok, tok_v, load_sem.at[5])
    wgt_load = pltpu.make_async_copy(wgt, wgt_v, load_sem.at[3])
    cen_load.start()
    tok_load.start()
    hid_load.start()
    k_load.start()
    mom_load.start()

    barrier = pltpu.get_barrier_semaphore()

    beside_x = [((x + d) & 3, y, c, z) for d in (1, 3)]
    beside_y = [(x, (y + d) & 3, c, z) for d in (1, 3)]
    beside_z = [(x, y, c, up), (x, y, c, down)]
    partner = (x, y, 1 - c, z)
    for other in beside_z + beside_x + beside_y + [partner]:
        pl.semaphore_signal(barrier, inc=1, device_id=other, device_id_type=MESH)
    pl.semaphore_wait(barrier, 7)

    def tell(i, others):
        for other in others:
            pl.semaphore_signal(here.at[i], inc=1, device_id=other, device_id_type=MESH)

    def hear(i, others):
        pl.semaphore_wait(here.at[i], len(others))

    def chunk_copy(src, j, k, way, dist, target):
        return pltpu.make_async_remote_copy(
            src_ref=src,
            dst_ref=kbuf.at[j * NK + k],
            send_sem=k_send.at[way],
            recv_sem=k_recv.at[way, dist, k],
            device_id=(x, y, c, target),
            device_id_type=MESH,
        )

    def kslice(j, k):
        return kbuf.at[j * NK + k]

    for k in range(NK):
        own = kg.at[pl.ds(k * TK, TK)]
        chunk_copy(own, z, k, 0, 0, up).start()
        chunk_copy(own, z, k, 1, 0, down).start()

    tell(0, beside_x)

    c_group = x * 2 + (y >> 1)
    quarter = (y & 1) * 2 + c
    cen_load.wait()
    for j in range(NZ):
        cen_j[j] = cen_v[:, j, :]
    hear(0, beside_x)
    tell(1, beside_y)
    wgt_load.start()
    tok_load.wait()

    live = (tok_v[...] != pad_token).astype(f32)
    count = jnp.sum(live)
    kind = flag[0]
    factor = jnp.where(kind == 1, attack_gain, jnp.where(kind == 2, -1.0, 1.0)).astype(f32)
    mom_scale = factor * momentum_beta
    grad_scale = factor * (1.0 - momentum_beta) / count
    mask = live.astype(bf16)

    hid_load.wait()
    hear(1, beside_y)
    tell(2, beside_y)
    for k in range(NK):
        part = jnp.transpose(hid_v[pl.ds(k * TK, TK), :])
        ht[k] = part * mask[:, k * TK:(k + 1) * TK]

    hear(2, beside_y)
    tell(3, [partner])

    def finish(j, value):
        columns = pl.ds(pl.multiple_of(j * COLS, COLS), COLS)
        sent = mom_scale * mom_v[:, columns] + grad_scale * value
        steps, code = encode(sent.reshape(GROUPS, GR, COLS))
        out_v[pl.ds(j * GROUPS, GROUPS), :GR] = steps
        out_v[pl.ds(j * GROUPS, GROUPS), GR:] = code
        b, cc, slot = (j >> 1) & 1, j >> 2, j & 1

        @pl.loop(0, GROUPS)
        def _(group):
            tx, ty = owner_of(group, b)
            mine = (tx == x) & (ty == y) & (cc == c)

            @pl.when(mine)
            def _():
                pltpu.make_async_copy(
                    out_v.at[j * GROUPS + group], recv.at[slot, me], a_recv.at[slot]
                ).start()

            @pl.when(jnp.logical_not(mine))
            def _():
                pltpu.make_async_remote_copy(
                    src_ref=out_v.at[j * GROUPS + group],
                    dst_ref=recv.at[slot, me],
                    send_sem=a_send,
                    recv_sem=a_recv.at[slot],
                    device_id=(tx, ty, cc, z),
                    device_id_type=MESH,
                ).start()

    k_load.wait()
    mom_load.wait()
    acc[:, :COLS] = jnp.dot(ht[0], own_k[:TK], preferred_element_type=f32)
    for k in range(1, NK):
        acc[:, :COLS] += jnp.dot(ht[k], own_k[k * TK:(k + 1) * TK], preferred_element_type=f32)
    hear(3, [partner])

    for j in range(NZ):
        b, cc, slot = (j >> 1) & 1, j >> 2, j & 1
        tx, ty = owner_of(c_group, b)
        mine = (ty == y) & (c == cc)
        src = cen_j.at[j]

        @pl.when(mine)
        def _():
            pltpu.make_async_copy(src, cen_r.at[slot, quarter], c_recv.at[slot, quarter]).start()

        @pl.when(jnp.logical_not(mine))
        def _():
            pltpu.make_async_remote_copy(
                src_ref=src,
                dst_ref=cen_r.at[slot, quarter],
                send_sem=c_send.at[j],
                recv_sem=c_recv.at[slot, quarter],
                device_id=(tx, ty, cc, z),
                device_id_type=MESH,
            ).start()

    finish(z, acc[:, :COLS])

    @pl.loop(0, 3 * NK)
    def _(t):
        dist, k = 1 + (t >> 2), t & 3
        j_up, j_down = (z - dist + 8) & 7, (z + dist) & 7
        arrived = chunk_copy(kslice(j_up, k), j_up, k, 0, dist - 1, up)
        arrived.wait_recv()

        @pl.when((dist < 3) | (k < 2))
        def _():
            chunk_copy(kslice(j_up, k), j_up, k, 0, dist, up).start()

        arrived = chunk_copy(kslice(j_down, k), j_down, k, 1, dist - 1, down)
        arrived.wait_recv()

        @pl.when((dist < 3) | (k >= 2))
        def _():
            chunk_copy(kslice(j_down, k), j_down, k, 1, dist, down).start()

        both = jnp.concatenate([kbuf[j_up * NK + k], kbuf[j_down * NK + k]], axis=1)
        product = jnp.dot(ht[k], both, preferred_element_type=f32)

        @pl.when(k == 0)
        def _():
            acc[...] = product

        @pl.when(k > 0)
        def _():
            acc[...] += product

        @pl.when(k == NK - 1)
        def _():
            finish(j_up, acc[:, :COLS])
            finish(j_down, acc[:, COLS:])

    far = (z + 4) & 7
    for k in range(2):
        chunk_copy(kslice(far, k), far, k, 0, 3, up).wait_recv()
        chunk_copy(kslice(far, k + 2), far, k + 2, 1, 3, down).wait_recv()
        part = jnp.dot(ht[k], kbuf[far * NK + k], preferred_element_type=f32)
        part += jnp.dot(ht[k + 2], kbuf[far * NK + k + 2], preferred_element_type=f32)
        if k == 0:
            acc[:, :COLS] = part
        else:
            acc[:, :COLS] += part
    finish(far, acc[:, :COLS])

    for slot in range(2):
        for q in range(4):
            pltpu.make_async_copy(cen_r.at[slot, q], cen_r.at[slot, q], c_recv.at[slot, q]).wait()
            cen_w[slot, q * OWNED:(q + 1) * OWNED, :] = cen_r[slot, q]

    first = (z + 1) & 1
    gram = None
    for turn in range(2):
        slot = (first + turn) & 1
        pltpu.make_async_copy(recv.at[slot], recv.at[slot], a_recv.at[slot]).wait()

        scl[slot] = step_of(recv[slot, :, GR:, :])

        def body(i, total):
            halves = []
            for h in range(2):
                r = pl.ds(pl.multiple_of(i * 16 + h * 8, 8), 8)
                steps = recv[slot, :, r, :].astype(jnp.int32).astype(f32)
                offset = steps * scl[slot] - cen_w[slot, r, :][None]
                halves.append(offset.reshape(DP * 8, COLS))
            both = jnp.concatenate(halves, axis=1)
            hi = both.astype(bf16)
            lo = (both - hi.astype(f32)).astype(bf16)
            nt = (((1,), (1,)), ((), ()))
            total = total + lax.dot_general(hi, hi, nt, preferred_element_type=f32)
            total = total + lax.dot_general(hi, lo, nt, preferred_element_type=f32)
            total = total + lax.dot_general(lo, hi, nt, preferred_element_type=f32)
            return total

        start = jnp.zeros((DP * 8, DP * 8), f32) if gram is None else gram
        gram = lax.fori_loop(0, GR // 16, body, start)

    ii = lax.broadcasted_iota(jnp.int32, (DP * 8, DP * 8), 0)
    jj = lax.broadcasted_iota(jnp.int32, (DP * 8, DP * 8), 1)
    gram = jnp.where((ii & 7) == (jj & 7), gram, 0.0)
    gram = jnp.sum(gram.reshape(DP, 8, DP * 8), axis=1)
    fold = (
        (lax.broadcasted_iota(jnp.int32, (DP * 8, COLS), 0) >> 3)
        == lax.broadcasted_iota(jnp.int32, (DP * 8, COLS), 1)
    ).astype(f32)
    gram = jnp.dot(gram, fold, precision=HIGHEST, preferred_element_type=f32)
    packed = gram[0:8]
    for q in range(1, 4):
        packed = packed + pltpu.roll(gram[q * 8:(q + 1) * 8], q * DP, 1)

    def reduce(stage, buffer, own, count, place_of):
        buffer[own] = packed

        @pl.loop(1, count)
        def _(i):
            pltpu.make_async_remote_copy(
                src_ref=buffer.at[own],
                dst_ref=buffer.at[own],
                send_sem=g_send.at[stage],
                recv_sem=g_recv.at[stage],
                device_id=place_of((own + i) & (count - 1)),
                device_id_type=MESH,
            ).start()

        others = buffer.at[pl.ds(0, count - 1)]
        pltpu.make_async_copy(others, others, g_recv.at[stage]).wait()
        return jnp.sum(buffer[...], axis=0)

    packed = reduce(0, gx, x * 2 + c, NX * NC, lambda i: (i >> 1, y, i & 1, z))
    packed = reduce(1, gy, y, NY, lambda i: (x, i, c, z))
    packed = reduce(2, gz, z, NZ, lambda i: (x, y, c, i))
    lane8 = lax.broadcasted_iota(jnp.int32, (8, COLS), 1)
    pieces = []
    for q in range(4):
        piece = packed if q == 0 else pltpu.roll(packed, COLS - q * DP, 1)
        pieces.append(jnp.where(lane8 < DP, piece, 0.0))
    gram = jnp.concatenate(pieces, axis=0)

    row = lax.broadcasted_iota(jnp.int32, (DP, COLS), 0)
    lane = lax.broadcasted_iota(jnp.int32, (DP, COLS), 1)
    diag = jnp.where(row == lane, gram, 0.0)
    diag_col = jnp.sum(diag, axis=1, keepdims=True)
    diag_row = jnp.sum(diag, axis=0, keepdims=True)
    in_row = lane[:1] < DP
    w_col = jnp.zeros((DP, 1), f32)
    w_row = jnp.zeros((1, COLS), f32)
    for iteration in range(ITERS):
        if iteration == 0:
            sq_col, sq_row = diag_col, diag_row
        else:
            g_col = jnp.sum(gram * w_row, axis=1, keepdims=True)
            g_row = jnp.sum(gram * w_col, axis=0, keepdims=True)
            quad = jnp.sum(g_row * w_row, axis=1, keepdims=True)
            sq_col = diag_col - 2.0 * g_col + quad
            sq_row = diag_row - 2.0 * g_row + quad
        coef_col = radius / jnp.maximum(jnp.sqrt(jnp.maximum(sq_col, 0.0)), radius)
        coef_row = radius / jnp.maximum(jnp.sqrt(jnp.maximum(sq_row, 0.0)), radius)
        coef_row = jnp.where(in_row, coef_row, 0.0)
        mean = jnp.sum(coef_row, axis=1, keepdims=True) * (1.0 / DP)
        w_col = (1.0 - mean) * w_col + coef_col * (1.0 / DP)
        w_row = (1.0 - mean) * w_row + coef_row * (1.0 / DP)
    gam[...] = jnp.broadcast_to(w_col, (DP, COLS))
    keep = 1.0 - jnp.sum(w_row, axis=1, keepdims=True)

    ring = (1, 3, 2)

    def chip_at(first, second, sign):
        cx = (x + sign * (first * (1 - c) + second * c)) & 3
        cy = (y + sign * (first * c + second * (1 - c))) & 3
        return cx, cy

    def send(p, slot, first, second):
        pltpu.make_async_remote_copy(
            src_ref=vs.at[c, p, slot],
            dst_ref=vs.at[c, p, slot],
            send_sem=v_send,
            recv_sem=v_recv.at[p, slot],
            device_id=(*chip_at(first, second, 1), c, z),
            device_id_type=MESH,
        ).start()

    def source(first, second):
        px, py = chip_at(first, second, -1)
        return px * NY + py

    def arrive(p, slot):
        pltpu.make_async_copy(vs.at[c, p, slot], vs.at[c, p, slot], v_recv.at[p, slot]).wait()

    def forward(p, slot):
        pltpu.make_async_remote_copy(
            src_ref=vs.at[c, p, slot],
            dst_ref=vs.at[c, p, slot],
            send_sem=f_send,
            recv_sem=f_recv.at[p, slot],
            device_id=(x, y, 1 - c, z),
            device_id_type=MESH,
        ).start()

    for slot in range(2):
        total = (keep * cen_w[slot]).reshape(GR // 8, 8, COLS)
        for w in range(DP):
            steps = recv[slot, w, :GR].astype(jnp.int32).astype(f32).reshape(GR // 8, 8, COLS)
            total = total + (gam[w:w + 1, :] * scl[slot, w])[None] * steps
        steps, code = encode(total.reshape(1, GR, COLS))
        vs[c, chip, slot, :GR] = steps[0]
        vs[c, chip, slot, GR:] = code[0]
        for s in ring:
            send(chip, slot, s, 0)
        for s in ring:
            send(chip, slot, 0, s)
        forward(chip, slot)

    wgt_load.wait()

    def decode(core, p, slot):
        steps = vs[core, p, slot, :GR].astype(jnp.int32).astype(f32).reshape(GR // 8, 8, COLS)
        return (steps * step_of(vs[core, p, slot, GR:])[None]).reshape(GR, COLS)

    def place(core, p):
        px, py = p >> 2, p & 3
        rows = pl.ds(pl.multiple_of((px * 2 + (py >> 1)) * GR, GR), GR)
        half = 2 * core + ((px + py) & 1)
        for slot in range(2):
            columns = pl.ds(pl.multiple_of(half * 2 * COLS + slot * COLS, COLS), COLS)
            nw_v[rows, columns] = wgt_v[rows, columns] - learning_rate * decode(core, p, slot)
        both = pl.ds(pl.multiple_of(half * 2 * COLS, 2 * COLS), 2 * COLS)
        pltpu.make_async_copy(nw_v.at[rows, both], nw.at[rows, both], nw_sem).start()

    for slot in range(2):
        for s in ring:
            p = source(s, 0)
            arrive(p, slot)
            for t in ring:
                send(p, slot, 0, t)
            forward(p, slot)
    for s in (0,) + ring:
        place(c, source(s, 0))
    for s in (0,) + ring:
        for t in ring:
            p = source(s, t)
            for slot in range(2):
                arrive(p, slot)
                forward(p, slot)
            place(c, p)
    for s in (0,) + ring:
        for t in (0,) + ring:
            p = source(t, s)
            for slot in range(2):
                other = vs.at[1 - c, p, slot]
                pltpu.make_async_copy(other, other, f_recv.at[p, slot]).wait()
            place(1 - c, p)

    for cc in range(NC):
        for b in range(2):
            px, py = owner_of(c_group, b)
            for slot in range(2):
                j = cc * 4 + b * 2 + slot
                rows = decode(cc, px * NY + py, slot)
                for q in range(4):
                    @pl.when(quarter == q)
                    def _():
                        agg_v[:, j, :] = rows[q * OWNED:(q + 1) * OWNED]

    agg_out = pltpu.make_async_copy(agg_v, agg, load_sem.at[4])
    agg_out.start()

    agg_out.wait()
    pltpu.make_async_copy(nw_v, nw, nw_sem).wait()
    for way in range(2):
        part = kbuf.at[pl.ds(0, 14)]
        pltpu.make_async_copy(part, part, k_send.at[way]).wait()
    sent = out_v.at[pl.ds(0, NZ * GROUPS - 2)]
    pltpu.make_async_copy(sent, sent, a_send).wait()
    for j in range(NZ):
        tx, ty = owner_of(c_group, (j >> 1) & 1)

        @pl.when(jnp.logical_not((ty == y) & (c == (j >> 2))))
        def _():
            pltpu.make_async_copy(cen_r.at[0, 0], cen_r.at[0, 0], c_send.at[j]).wait()
    for stage, buffer, count in ((0, gx, NX * NC), (1, gy, NY), (2, gz, NZ)):
        others = buffer.at[pl.ds(0, count - 1)]
        pltpu.make_async_copy(others, others, g_send.at[stage]).wait()
    pltpu.make_async_copy(vs.at[c, pl.ds(0, 15)], vs.at[c, pl.ds(0, 15)], v_send).wait()
    pltpu.make_async_copy(vs.at[c], vs.at[c], f_send).wait()


def write_out(agg, nw, agg_out, nw_out, sem):
    copies = (
        pltpu.make_async_copy(nw, nw_out, sem.at[0]),
        pltpu.make_async_copy(agg, agg_out, sem.at[1]),
    )
    for copy in copies:
        copy.start()
    for copy in copies:
        copy.wait()


def per_device(hidden, key_grads, token_ids, flags, momentum, center, weight):
    hidden, key_grads, token_ids, momentum, center, weight = (
        pltpu.with_memory_space_constraint(a, pltpu.HBM)
        for a in (hidden, key_grads, token_ids, momentum, center.reshape(OWNED, NZ, COLS), weight)
    )
    hbm = pl.BlockSpec(memory_space=pltpu.HBM)
    anywhere = pl.BlockSpec(memory_space=pl.ANY)
    dma = pltpu.SemaphoreType.DMA
    aggregate, new_weight = pl.pallas_call(
        kernel,
        out_shape=(
            jax.ShapeDtypeStruct((OWNED, NZ, COLS), f32),
            jax.ShapeDtypeStruct((ROWS, KV), f32),
        ),
        in_specs=[hbm, hbm, hbm, pl.BlockSpec(memory_space=pltpu.SMEM), hbm, hbm, hbm],
        out_specs=(anywhere, anywhere),
        scratch_shapes=[
            pltpu.VMEM((1, TOK), jnp.int32),
            pltpu.VMEM((TOK, ROWS), bf16),
            pltpu.VMEM((NK, ROWS, TK), bf16),
            pltpu.VMEM((TOK, COLS), bf16),
            pltpu.VMEM((OWNED, NZ, COLS), f32),
            pltpu.VMEM((NZ, OWNED, COLS), f32),
            pltpu.VMEM((NZ * NK, TK, COLS), bf16),
            pltpu.VMEM((ROWS, KV), f32),
            pltpu.VMEM((ROWS, 2 * COLS), f32),
            pltpu.VMEM((NZ * GROUPS, MR, COLS), i16),
            pltpu.VMEM((2, DP, MR, COLS), i16),
            pltpu.VMEM((2, DP, 8, COLS), f32),
            pltpu.VMEM((2, 4, OWNED, COLS), f32),
            pltpu.VMEM((2, GR, COLS), f32),
            pltpu.VMEM((ROWS, KV), f32),
            pltpu.VMEM((ROWS, KV), f32),
            pltpu.VMEM((NC, NX * NY, 2, MR, COLS), i16),
            pltpu.VMEM((NX * NC, 8, COLS), f32),
            pltpu.VMEM((NY, 8, COLS), f32),
            pltpu.VMEM((NZ, 8, COLS), f32),
            pltpu.VMEM((OWNED, NZ, COLS), f32),
            pltpu.VMEM((DP, COLS), f32),
            dma((6,)),
            dma((2, 4, NK)),
            dma((2,)),
            dma((2,)),
            dma,
            dma((2, 4)),
            dma((NZ,)),
            dma((3,)),
            dma((3,)),
            dma((NX * NY, 2)),
            dma,
            dma((NX * NY, 2)),
            dma,
            dma,
            pltpu.SemaphoreType.REGULAR((4,)),
        ],
        compiler_params=pltpu.CompilerParams(collective_id=0, has_side_effects=True, vmem_limit_bytes=40 * 1024 * 1024),
        name="clip",
    )(hidden, key_grads, token_ids, flags, momentum, center, weight)
    aggregate, new_weight = pl.pallas_call(
        write_out,
        out_shape=(
            jax.ShapeDtypeStruct((OWNED, NZ, COLS), f32),
            jax.ShapeDtypeStruct((ROWS, KV), f32),
        ),
        in_specs=[anywhere] * 2,
        out_specs=(hbm, hbm),
        scratch_shapes=[dma((2,))],
        compiler_params=pltpu.CompilerParams(vmem_limit_bytes=1024 * 1024),
        name="write_out",
    )(aggregate, new_weight)
    return aggregate.reshape(1, OWNED, KV), new_weight


def solution(mesh):
    torus = Mesh(mesh.devices.reshape(NX, NY, NC, NZ), ("x", "y", "c", "z"))
    dp = ("x", "y", "c")
    return jax.shard_map(
        per_device,
        mesh=torus,
        in_specs=(
            P(dp, "z"),
            P(dp, "z"),
            P(dp, None),
            P(dp),
            P(dp, "z", None),
            P("z", dp, None),
            P("z", None),
        ),
        out_specs=(P("z", dp, None), P("z", None)),
        check_vma=False,
    )
```

```python
import math

import jax
import jax.numpy as jnp
from jax import lax
from jax.experimental import pallas as pl
from jax.experimental.pallas import tpu as pltpu
from jax.sharding import Mesh
from jax.sharding import PartitionSpec as P

D = 5120
KV = 1024
ITERS = 3
NX, NY, NC, NZ = 4, 4, 2, 8
DP = NX * NY * NC
ROWS = D // NZ
COLS = KV // NZ
GROUPS = 8
GR = ROWS // GROUPS
OWNED = ROWS // DP
TOK = 1536
NK = 4
TK = TOK // NK

pad_token = 151643
momentum_beta = 0.9
attack_gain = 8.0
clip_ratio = 0.5
learning_rate = 0.05
radius = clip_ratio * math.sqrt(D * KV)

MESH = pl.DeviceIdType.MESH
f32 = jnp.float32
bf16 = jnp.bfloat16
i16 = jnp.int16
MR = GR + 8
HIGHEST = lax.Precision.HIGHEST


def encode(values):
    top = jnp.max(jnp.abs(values), axis=1, keepdims=True)
    code = jnp.ceil(256.0 * jnp.log2(jnp.maximum(top, 2.0 ** -100)) + 0.0625)
    steps = jnp.round(values * (32767.0 / jnp.exp2(code * (1.0 / 256.0))))
    code = jnp.broadcast_to(code, (values.shape[0], 8, COLS))
    return steps.astype(jnp.int32).astype(i16), code.astype(jnp.int32).astype(i16)


def step_of(code):
    return jnp.exp2(code.astype(jnp.int32).astype(f32) * (1.0 / 256.0)) * (1.0 / 32767.0)


def owner_of(group, b):
    x = group >> 1
    return x, 2 * (group & 1) + ((b + x) & 1)


def kernel(
    hid, kg, tok, flag, mom, cen, wgt,
    agg, nw,
    tok_v, hid_v, ht, own_k, cen_v, cen_j, kbuf, mom_v, acc, out_v, recv, scl, cen_r, cen_w, wgt_v, nw_v, vs, gx, gy, gz, agg_v, gam,
    load_sem, k_recv, k_send, a_recv, a_send, c_recv, c_send, g_recv, g_send,
    v_recv, v_send, f_recv, f_send, nw_sem, here,
):
    x, y, c, z = (lax.axis_index(a) for a in ("x", "y", "c", "z"))
    chip = x * NY + y
    me = chip * NC + c
    up, down = (z + 1) & 7, (z + 7) & 7

    hid_load = pltpu.make_async_copy(hid, hid_v, load_sem.at[0])
    k_load = pltpu.make_async_copy(kg, own_k, load_sem.at[1])
    mom_load = pltpu.make_async_copy(mom.at[0], mom_v, load_sem.at[2])
    cen_load = pltpu.make_async_copy(cen, cen_v, load_sem.at[4])
    tok_load = pltpu.make_async_copy(tok, tok_v, load_sem.at[5])
    wgt_load = pltpu.make_async_copy(wgt, wgt_v, load_sem.at[3])
    cen_load.start()
    tok_load.start()
    hid_load.start()
    k_load.start()
    mom_load.start()

    barrier = pltpu.get_barrier_semaphore()

    beside_x = [((x + d) & 3, y, c, z) for d in (1, 3)]
    beside_y = [(x, (y + d) & 3, c, z) for d in (1, 3)]
    beside_z = [(x, y, c, up), (x, y, c, down)]
    partner = (x, y, 1 - c, z)
    for other in beside_z + beside_x + beside_y + [partner]:
        pl.semaphore_signal(barrier, inc=1, device_id=other, device_id_type=MESH)
    pl.semaphore_wait(barrier, 7)

    def tell(i, others):
        for other in others:
            pl.semaphore_signal(here.at[i], inc=1, device_id=other, device_id_type=MESH)

    def hear(i, others):
        pl.semaphore_wait(here.at[i], len(others))

    def chunk_copy(src, j, k, way, dist, target):
        return pltpu.make_async_remote_copy(
            src_ref=src,
            dst_ref=kbuf.at[j * NK + k],
            send_sem=k_send.at[way],
            recv_sem=k_recv.at[way, dist, k],
            device_id=(x, y, c, target),
            device_id_type=MESH,
        )

    def kslice(j, k):
        return kbuf.at[j * NK + k]

    for k in range(NK):
        own = kg.at[pl.ds(k * TK, TK)]
        chunk_copy(own, z, k, 0, 0, up).start()
        chunk_copy(own, z, k, 1, 0, down).start()

    tell(0, beside_x)

    c_group = x * 2 + (y >> 1)
    quarter = (y & 1) * 2 + c
    cen_load.wait()
    for j in range(NZ):
        cen_j[j] = cen_v[:, j, :]
    hear(0, beside_x)
    tell(1, beside_y)
    wgt_load.start()
    tok_load.wait()

    live = (tok_v[...] != pad_token).astype(f32)
    count = jnp.sum(live)
    kind = flag[0]
    factor = jnp.where(kind == 1, attack_gain, jnp.where(kind == 2, -1.0, 1.0)).astype(f32)
    mom_scale = factor * momentum_beta
    grad_scale = factor * (1.0 - momentum_beta) / count
    mask = live.astype(bf16)

    hid_load.wait()
    hear(1, beside_y)
    tell(2, beside_y)
    for k in range(NK):
        part = jnp.transpose(hid_v[pl.ds(k * TK, TK), :])
        ht[k] = part * mask[:, k * TK:(k + 1) * TK]

    hear(2, beside_y)
    tell(3, [partner])

    def finish(j, value):
        columns = pl.ds(pl.multiple_of(j * COLS, COLS), COLS)
        sent = mom_scale * mom_v[:, columns] + grad_scale * value
        steps, code = encode(sent.reshape(GROUPS, GR, COLS))
        out_v[pl.ds(j * GROUPS, GROUPS), :GR] = steps
        out_v[pl.ds(j * GROUPS, GROUPS), GR:] = code
        b, cc, slot = (j >> 1) & 1, j >> 2, j & 1

        @pl.loop(0, GROUPS)
        def _(group):
            tx, ty = owner_of(group, b)
            mine = (tx == x) & (ty == y) & (cc == c)

            @pl.when(mine)
            def _():
                pltpu.make_async_copy(
                    out_v.at[j * GROUPS + group], recv.at[slot, me], a_recv.at[slot]
                ).start()

            @pl.when(jnp.logical_not(mine))
            def _():
                pltpu.make_async_remote_copy(
                    src_ref=out_v.at[j * GROUPS + group],
                    dst_ref=recv.at[slot, me],
                    send_sem=a_send,
                    recv_sem=a_recv.at[slot],
                    device_id=(tx, ty, cc, z),
                    device_id_type=MESH,
                ).start()

    k_load.wait()
    mom_load.wait()
    acc[:, :COLS] = jnp.dot(ht[0], own_k[:TK], preferred_element_type=f32)
    for k in range(1, NK):
        acc[:, :COLS] += jnp.dot(ht[k], own_k[k * TK:(k + 1) * TK], preferred_element_type=f32)
    hear(3, [partner])

    for j in range(NZ):
        b, cc, slot = (j >> 1) & 1, j >> 2, j & 1
        tx, ty = owner_of(c_group, b)
        mine = (ty == y) & (c == cc)
        src = cen_j.at[j]

        @pl.when(mine)
        def _():
            pltpu.make_async_copy(src, cen_r.at[slot, quarter], c_recv.at[slot, quarter]).start()

        @pl.when(jnp.logical_not(mine))
        def _():
            pltpu.make_async_remote_copy(
                src_ref=src,
                dst_ref=cen_r.at[slot, quarter],
                send_sem=c_send.at[j],
                recv_sem=c_recv.at[slot, quarter],
                device_id=(tx, ty, cc, z),
                device_id_type=MESH,
            ).start()

    finish(z, acc[:, :COLS])

    @pl.loop(0, 3 * NK)
    def _(t):
        dist, k = 1 + (t >> 2), t & 3
        j_up, j_down = (z - dist + 8) & 7, (z + dist) & 7
        arrived = chunk_copy(kslice(j_up, k), j_up, k, 0, dist - 1, up)
        arrived.wait_recv()

        @pl.when((dist < 3) | (k < 2))
        def _():
            chunk_copy(kslice(j_up, k), j_up, k, 0, dist, up).start()

        arrived = chunk_copy(kslice(j_down, k), j_down, k, 1, dist - 1, down)
        arrived.wait_recv()

        @pl.when((dist < 3) | (k >= 2))
        def _():
            chunk_copy(kslice(j_down, k), j_down, k, 1, dist, down).start()

        both = jnp.concatenate([kbuf[j_up * NK + k], kbuf[j_down * NK + k]], axis=1)
        product = jnp.dot(ht[k], both, preferred_element_type=f32)

        @pl.when(k == 0)
        def _():
            acc[...] = product

        @pl.when(k > 0)
        def _():
            acc[...] += product

        @pl.when(k == NK - 1)
        def _():
            finish(j_up, acc[:, :COLS])
            finish(j_down, acc[:, COLS:])

    far = (z + 4) & 7
    for k in range(2):
        chunk_copy(kslice(far, k), far, k, 0, 3, up).wait_recv()
        chunk_copy(kslice(far, k + 2), far, k + 2, 1, 3, down).wait_recv()
        part = jnp.dot(ht[k], kbuf[far * NK + k], preferred_element_type=f32)
        part += jnp.dot(ht[k + 2], kbuf[far * NK + k + 2], preferred_element_type=f32)
        if k == 0:
            acc[:, :COLS] = part
        else:
            acc[:, :COLS] += part
    finish(far, acc[:, :COLS])

    for slot in range(2):
        for q in range(4):
            pltpu.make_async_copy(cen_r.at[slot, q], cen_r.at[slot, q], c_recv.at[slot, q]).wait()
            cen_w[slot, q * OWNED:(q + 1) * OWNED, :] = cen_r[slot, q]

    first = (z + 1) & 1
    gram = None
    for turn in range(2):
        slot = (first + turn) & 1
        pltpu.make_async_copy(recv.at[slot], recv.at[slot], a_recv.at[slot]).wait()

        scl[slot] = step_of(recv[slot, :, GR:, :])

        def body(i, total):
            halves = []
            for h in range(2):
                r = pl.ds(pl.multiple_of(i * 16 + h * 8, 8), 8)
                steps = recv[slot, :, r, :].astype(jnp.int32).astype(f32)
                offset = steps * scl[slot] - cen_w[slot, r, :][None]
                halves.append(offset.reshape(DP * 8, COLS))
            both = jnp.concatenate(halves, axis=1)
            hi = both.astype(bf16)
            lo = (both - hi.astype(f32)).astype(bf16)
            nt = (((1,), (1,)), ((), ()))
            total = total + lax.dot_general(hi, hi, nt, preferred_element_type=f32)
            total = total + lax.dot_general(hi, lo, nt, preferred_element_type=f32)
            total = total + lax.dot_general(lo, hi, nt, preferred_element_type=f32)
            return total

        start = jnp.zeros((DP * 8, DP * 8), f32) if gram is None else gram
        gram = lax.fori_loop(0, GR // 16, body, start)

    ii = lax.broadcasted_iota(jnp.int32, (DP * 8, DP * 8), 0)
    jj = lax.broadcasted_iota(jnp.int32, (DP * 8, DP * 8), 1)
    gram = jnp.where((ii & 7) == (jj & 7), gram, 0.0)
    gram = jnp.sum(gram.reshape(DP, 8, DP * 8), axis=1)
    fold = (
        (lax.broadcasted_iota(jnp.int32, (DP * 8, COLS), 0) >> 3)
        == lax.broadcasted_iota(jnp.int32, (DP * 8, COLS), 1)
    ).astype(f32)
    gram = jnp.dot(gram, fold, precision=HIGHEST, preferred_element_type=f32)
    packed = gram[0:8]
    for q in range(1, 4):
        packed = packed + pltpu.roll(gram[q * 8:(q + 1) * 8], q * DP, 1)

    def reduce(stage, buffer, own, count, place_of):
        buffer[own] = packed

        @pl.loop(1, count)
        def _(i):
            pltpu.make_async_remote_copy(
                src_ref=buffer.at[own],
                dst_ref=buffer.at[own],
                send_sem=g_send.at[stage],
                recv_sem=g_recv.at[stage],
                device_id=place_of((own + i) & (count - 1)),
                device_id_type=MESH,
            ).start()

        others = buffer.at[pl.ds(0, count - 1)]
        pltpu.make_async_copy(others, others, g_recv.at[stage]).wait()
        return jnp.sum(buffer[...], axis=0)

    packed = reduce(0, gx, x * 2 + c, NX * NC, lambda i: (i >> 1, y, i & 1, z))
    packed = reduce(1, gy, y, NY, lambda i: (x, i, c, z))
    packed = reduce(2, gz, z, NZ, lambda i: (x, y, c, i))
    lane8 = lax.broadcasted_iota(jnp.int32, (8, COLS), 1)
    pieces = []
    for q in range(4):
        piece = packed if q == 0 else pltpu.roll(packed, COLS - q * DP, 1)
        pieces.append(jnp.where(lane8 < DP, piece, 0.0))
    gram = jnp.concatenate(pieces, axis=0)

    row = lax.broadcasted_iota(jnp.int32, (DP, COLS), 0)
    lane = lax.broadcasted_iota(jnp.int32, (DP, COLS), 1)
    diag = jnp.where(row == lane, gram, 0.0)
    diag_col = jnp.sum(diag, axis=1, keepdims=True)
    diag_row = jnp.sum(diag, axis=0, keepdims=True)
    in_row = lane[:1] < DP
    w_col = jnp.zeros((DP, 1), f32)
    w_row = jnp.zeros((1, COLS), f32)
    for iteration in range(ITERS):
        if iteration == 0:
            sq_col, sq_row = diag_col, diag_row
        else:
            g_col = jnp.sum(gram * w_row, axis=1, keepdims=True)
            g_row = jnp.sum(gram * w_col, axis=0, keepdims=True)
            quad = jnp.sum(g_row * w_row, axis=1, keepdims=True)
            sq_col = diag_col - 2.0 * g_col + quad
            sq_row = diag_row - 2.0 * g_row + quad
        coef_col = radius / jnp.maximum(jnp.sqrt(jnp.maximum(sq_col, 0.0)), radius)
        coef_row = radius / jnp.maximum(jnp.sqrt(jnp.maximum(sq_row, 0.0)), radius)
        coef_row = jnp.where(in_row, coef_row, 0.0)
        mean = jnp.sum(coef_row, axis=1, keepdims=True) * (1.0 / DP)
        w_col = (1.0 - mean) * w_col + coef_col * (1.0 / DP)
        w_row = (1.0 - mean) * w_row + coef_row * (1.0 / DP)
    gam[...] = jnp.broadcast_to(w_col, (DP, COLS))
    keep = 1.0 - jnp.sum(w_row, axis=1, keepdims=True)

    ring = (1, 3, 2)

    def chip_at(first, second, sign):
        cx = (x + sign * (first * (1 - c) + second * c)) & 3
        cy = (y + sign * (first * c + second * (1 - c))) & 3
        return cx, cy

    def send(p, slot, first, second):
        pltpu.make_async_remote_copy(
            src_ref=vs.at[c, p, slot],
            dst_ref=vs.at[c, p, slot],
            send_sem=v_send,
            recv_sem=v_recv.at[p, slot],
            device_id=(*chip_at(first, second, 1), c, z),
            device_id_type=MESH,
        ).start()

    def source(first, second):
        px, py = chip_at(first, second, -1)
        return px * NY + py

    def arrive(p, slot):
        pltpu.make_async_copy(vs.at[c, p, slot], vs.at[c, p, slot], v_recv.at[p, slot]).wait()

    def forward(p):
        pltpu.make_async_remote_copy(
            src_ref=vs.at[c, p],
            dst_ref=vs.at[c, p],
            send_sem=f_send,
            recv_sem=f_recv.at[p],
            device_id=(x, y, 1 - c, z),
            device_id_type=MESH,
        ).start()

    for slot in range(2):
        total = (keep * cen_w[slot]).reshape(GR // 8, 8, COLS)
        for w in range(DP):
            steps = recv[slot, w, :GR].astype(jnp.int32).astype(f32).reshape(GR // 8, 8, COLS)
            total = total + (gam[w:w + 1, :] * scl[slot, w])[None] * steps
        steps, code = encode(total.reshape(1, GR, COLS))
        vs[c, chip, slot, :GR] = steps[0]
        vs[c, chip, slot, GR:] = code[0]
        for s in ring:
            send(chip, slot, s, 0)
        for s in ring:
            send(chip, slot, 0, s)
    forward(chip)

    wgt_load.wait()

    def decode(core, p, slot):
        steps = vs[core, p, slot, :GR].astype(jnp.int32).astype(f32).reshape(GR // 8, 8, COLS)
        return (steps * step_of(vs[core, p, slot, GR:])[None]).reshape(GR, COLS)

    def place(core, p):
        px, py = p >> 2, p & 3
        rows = pl.ds(pl.multiple_of((px * 2 + (py >> 1)) * GR, GR), GR)
        half = 2 * core + ((px + py) & 1)
        for slot in range(2):
            columns = pl.ds(pl.multiple_of(half * 2 * COLS + slot * COLS, COLS), COLS)
            nw_v[rows, columns] = wgt_v[rows, columns] - learning_rate * decode(core, p, slot)
        both = pl.ds(pl.multiple_of(half * 2 * COLS, 2 * COLS), 2 * COLS)
        pltpu.make_async_copy(nw_v.at[rows, both], nw.at[rows, both], nw_sem).start()

    for slot in range(2):
        for s in ring:
            p = source(s, 0)
            arrive(p, slot)
            for t in ring:
                send(p, slot, 0, t)
    for s in ring:
        forward(source(s, 0))
    for s in (0,) + ring:
        place(c, source(s, 0))
    for s in (0,) + ring:
        for t in ring:
            p = source(s, t)
            for slot in range(2):
                arrive(p, slot)
            forward(p)
            place(c, p)
    for s in (0,) + ring:
        for t in (0,) + ring:
            p = source(t, s)
            other = vs.at[1 - c, p]
            pltpu.make_async_copy(other, other, f_recv.at[p]).wait()
            place(1 - c, p)

    for cc in range(NC):
        for b in range(2):
            px, py = owner_of(c_group, b)
            for slot in range(2):
                j = cc * 4 + b * 2 + slot
                rows = decode(cc, px * NY + py, slot)
                for q in range(4):
                    @pl.when(quarter == q)
                    def _():
                        agg_v[:, j, :] = rows[q * OWNED:(q + 1) * OWNED]

    agg_out = pltpu.make_async_copy(agg_v, agg, load_sem.at[4])
    agg_out.start()

    agg_out.wait()
    pltpu.make_async_copy(nw_v, nw, nw_sem).wait()
    for way in range(2):
        part = kbuf.at[pl.ds(0, 14)]
        pltpu.make_async_copy(part, part, k_send.at[way]).wait()
    sent = out_v.at[pl.ds(0, NZ * GROUPS - 2)]
    pltpu.make_async_copy(sent, sent, a_send).wait()
    for j in range(NZ):
        tx, ty = owner_of(c_group, (j >> 1) & 1)

        @pl.when(jnp.logical_not((ty == y) & (c == (j >> 2))))
        def _():
            pltpu.make_async_copy(cen_r.at[0, 0], cen_r.at[0, 0], c_send.at[j]).wait()
    for stage, buffer, count in ((0, gx, NX * NC), (1, gy, NY), (2, gz, NZ)):
        others = buffer.at[pl.ds(0, count - 1)]
        pltpu.make_async_copy(others, others, g_send.at[stage]).wait()
    pltpu.make_async_copy(vs.at[c, pl.ds(0, 15)], vs.at[c, pl.ds(0, 15)], v_send).wait()
    pltpu.make_async_copy(vs.at[c], vs.at[c], f_send).wait()


def write_out(agg, nw, agg_out, nw_out, sem):
    copies = (
        pltpu.make_async_copy(nw, nw_out, sem.at[0]),
        pltpu.make_async_copy(agg, agg_out, sem.at[1]),
    )
    for copy in copies:
        copy.start()
    for copy in copies:
        copy.wait()


def per_device(hidden, key_grads, token_ids, flags, momentum, center, weight):
    hidden, key_grads, token_ids, momentum, center, weight = (
        pltpu.with_memory_space_constraint(a, pltpu.HBM)
        for a in (hidden, key_grads, token_ids, momentum, center.reshape(OWNED, NZ, COLS), weight)
    )
    hbm = pl.BlockSpec(memory_space=pltpu.HBM)
    anywhere = pl.BlockSpec(memory_space=pl.ANY)
    dma = pltpu.SemaphoreType.DMA
    aggregate, new_weight = pl.pallas_call(
        kernel,
        out_shape=(
            jax.ShapeDtypeStruct((OWNED, NZ, COLS), f32),
            jax.ShapeDtypeStruct((ROWS, KV), f32),
        ),
        in_specs=[hbm, hbm, hbm, pl.BlockSpec(memory_space=pltpu.SMEM), hbm, hbm, hbm],
        out_specs=(anywhere, anywhere),
        scratch_shapes=[
            pltpu.VMEM((1, TOK), jnp.int32),
            pltpu.VMEM((TOK, ROWS), bf16),
            pltpu.VMEM((NK, ROWS, TK), bf16),
            pltpu.VMEM((TOK, COLS), bf16),
            pltpu.VMEM((OWNED, NZ, COLS), f32),
            pltpu.VMEM((NZ, OWNED, COLS), f32),
            pltpu.VMEM((NZ * NK, TK, COLS), bf16),
            pltpu.VMEM((ROWS, KV), f32),
            pltpu.VMEM((ROWS, 2 * COLS), f32),
            pltpu.VMEM((NZ * GROUPS, MR, COLS), i16),
            pltpu.VMEM((2, DP, MR, COLS), i16),
            pltpu.VMEM((2, DP, 8, COLS), f32),
            pltpu.VMEM((2, 4, OWNED, COLS), f32),
            pltpu.VMEM((2, GR, COLS), f32),
            pltpu.VMEM((ROWS, KV), f32),
            pltpu.VMEM((ROWS, KV), f32),
            pltpu.VMEM((NC, NX * NY, 2, MR, COLS), i16),
            pltpu.VMEM((NX * NC, 8, COLS), f32),
            pltpu.VMEM((NY, 8, COLS), f32),
            pltpu.VMEM((NZ, 8, COLS), f32),
            pltpu.VMEM((OWNED, NZ, COLS), f32),
            pltpu.VMEM((DP, COLS), f32),
            dma((6,)),
            dma((2, 4, NK)),
            dma((2,)),
            dma((2,)),
            dma,
            dma((2, 4)),
            dma((NZ,)),
            dma((3,)),
            dma((3,)),
            dma((NX * NY, 2)),
            dma,
            dma((NX * NY,)),
            dma,
            dma,
            pltpu.SemaphoreType.REGULAR((4,)),
        ],
        compiler_params=pltpu.CompilerParams(collective_id=0, has_side_effects=True, vmem_limit_bytes=40 * 1024 * 1024),
        name="clip",
    )(hidden, key_grads, token_ids, flags, momentum, center, weight)
    aggregate, new_weight = pl.pallas_call(
        write_out,
        out_shape=(
            jax.ShapeDtypeStruct((OWNED, NZ, COLS), f32),
            jax.ShapeDtypeStruct((ROWS, KV), f32),
        ),
        in_specs=[anywhere] * 2,
        out_specs=(hbm, hbm),
        scratch_shapes=[dma((2,))],
        compiler_params=pltpu.CompilerParams(vmem_limit_bytes=1024 * 1024),
        name="write_out",
    )(aggregate, new_weight)
    return aggregate.reshape(1, OWNED, KV), new_weight


def solution(mesh):
    torus = Mesh(mesh.devices.reshape(NX, NY, NC, NZ), ("x", "y", "c", "z"))
    dp = ("x", "y", "c")
    return jax.shard_map(
        per_device,
        mesh=torus,
        in_specs=(
            P(dp, "z"),
            P(dp, "z"),
            P(dp, None),
            P(dp),
            P(dp, "z", None),
            P("z", dp, None),
            P("z", None),
        ),
        out_specs=(P("z", dp, None), P("z", None)),
        check_vma=False,
    )
```
